32 devices in a mesh: prompts: 2 (over x), beam: 16 (over z, y, core).
Axes of the slice: x: 2, y: 2, z: 4, core: 2. Of those that a mesh axis runs over, the one named last changes fastest.
Arguments:
- queries: bfloat16 [128, 256, 4096], P(('prompts', 'beam')), parts along dimension 0, may hold values from -4.375 to 4.375
- new_keys: bfloat16 [128, 256, 1024], P(('prompts', 'beam')), parts along dimension 0, may hold values from -4.375 to 4.375
- new_values: bfloat16 [128, 256, 1024], P(('prompts', 'beam')), parts along dimension 0, may hold values from -6 to 6
- step_kv: bfloat16 [128, 2, 64, 1024], P(('prompts', 'beam')), parts along dimension 0, may hold values from -6 to 6
- prm_last: bfloat16 [128, 4096], P(('prompts', 'beam')), parts along dimension 0, may hold values from -6 to 6
- value_head: float32 [4096], replicated, may hold values from -0.09375 to 0.09375
- parents: int32 [128], P('prompts'), parts along dimension 0, may hold values from 0 to 63, as said below
Outputs:
- attended: bfloat16 [128, 256, 4096], P(('prompts', 'beam')), parts along dimension 0
- child_share: float32 [128], P(('prompts', 'beam')), parts along dimension 0
The draws below stay inside these ranges and needn't reach their ends.
There are 2 independent parts, one for each index of `prompts`. The reference program is written for one: setup_inputs(seed, part) draws one part's arguments, and reference() takes and returns one part's arrays. A program takes and returns all parts, laid end to end along the dimension named above; an argument that names none is the same for every part. Nothing has to cross between parts.
Inputs may be any that keep to these rules, and one draw needn't show every extreme that they name: `parents`: on every device exactly 2 of its 4 beams are the parent of one or more children and the other beams of none.
All inputs are finite; a program needn't handle non-finite values.
Results may differ from the reference program's by a relative error of at most 0.008.
Values may be sent and summed in bfloat16 or wider, within the bound.
A program may use at most 192 MiB of HBM per device.

```python
import jax
import jax.numpy as jnp
from jax import lax

D = 4096
HEADS = 32
KV_HEADS = 8
HEAD_SIZE = 128
NEW = 256
STEP = 64
BEAM_DEV = 4
KEEP = 2
BEAMS = 64
CHILDREN = 64


def drawn_pair(key):
    base = jax.random.fold_in(key, 7919)
    key_q, key_k = jax.random.split(base, 2)
    q_shape = (CHILDREN, NEW, HEADS * HEAD_SIZE)
    k_shape = (CHILDREN, NEW, KV_HEADS * HEAD_SIZE)
    queries = jnp.clip(jax.random.normal(key_q, q_shape, jnp.float32), -4.375, 4.375)
    keys = jnp.clip(jax.random.normal(key_k, k_shape, jnp.float32), -4.375, 4.375)
    return (queries, keys)


def draw_queries(key, part):
    return drawn_pair(key)[0].astype(jnp.bfloat16)


def draw_new_keys(key, part):
    return drawn_pair(key)[1].astype(jnp.bfloat16)


def draw_parents(key, part):
    base = jax.random.fold_in(key, 5303)
    key_a, key_b, key_c, key_d, key_e = jax.random.split(base, 5)
    groups = BEAMS // BEAM_DEV
    ranks = jax.random.randint(key_a, (groups, BEAM_DEV), 0, 1048576) * BEAM_DEV + jnp.arange(BEAM_DEV)[None, :]
    order = jnp.argsort(ranks, axis=1, stable=True)
    kept_beams = (jnp.arange(groups)[:, None] * BEAM_DEV + order[:, :KEEP]).reshape(-1)
    kept_count = groups * KEEP
    shuffled = jax.random.permutation(key_b, kept_beams)
    extra = CHILDREN - kept_count
    upper = jax.random.randint(key_c, (extra,), 1, kept_count + 1)
    picks = jax.random.randint(key_d, (extra,), 0, upper)
    assign = jnp.concatenate([shuffled, shuffled[picks]])
    return jax.random.permutation(key_e, assign).astype(jnp.int32)


def shard_levels(rng, dims, cuts, smallest, high):
    level, own = 1.0, jax.random.fold_in(rng, 6)
    for position, parts in cuts:
        draws = jnp.exp(jax.random.uniform(jax.random.fold_in(own, position), (parts,), jnp.float32, smallest / len(cuts), high / len(cuts)))
        level = level * jnp.repeat(draws, dims[position] // parts).reshape([-1 if axis == position else 1 for axis in range(len(dims))])
    return level


def centred(key, dims, deviation, most, cuts=(), held_as=jnp.bfloat16):
    level = shard_levels(key, dims, cuts, -0.22, 0.18) if cuts else 1.0
    entries = jax.random.normal(key, dims, jnp.float32) * deviation * level
    return jnp.minimum(jnp.maximum(entries, -most), most).astype(held_as)


def setup_inputs(seed: int = 0, part: int = 0) -> dict:
    key_list = jax.random.split(jax.random.key(seed), 8)
    part_keys = jax.random.split(jax.random.fold_in(key_list[7], part), 8)
    queries = draw_queries(jax.random.fold_in(jax.random.fold_in(key_list[7], part), 71), part)
    new_keys = draw_new_keys(jax.random.fold_in(jax.random.fold_in(key_list[7], part), 71), part)
    new_values = centred(part_keys[2], (CHILDREN, NEW, KV_HEADS * HEAD_SIZE), 1.0, 6.0, ((0, 16),))
    step_kv = centred(part_keys[3], (BEAMS, 2, STEP, KV_HEADS * HEAD_SIZE), 1.0, 6.0, ((0, 16),))
    prm_last = centred(part_keys[4], (BEAMS, D), 1.0, 6.0, ((0, 16),))
    value_head = centred(key_list[5], (D,), D ** -0.5, 0.09375, (), jnp.float32)
    parents = draw_parents(jax.random.fold_in(jax.random.fold_in(key_list[7], part), 71), part)
    return dict(queries=queries, new_keys=new_keys, new_values=new_values, step_kv=step_kv, prm_last=prm_last, value_head=value_head, parents=parents)


def attend_child(operands):
    query, keys, values = operands
    total_len = keys.shape[0]
    new_len = query.shape[0]
    step_len = total_len - new_len
    kv_width = keys.shape[1]
    kv_heads = kv_width // HEAD_SIZE
    group = query.shape[1] // kv_width
    query_head_rows = query.astype(jnp.float32).reshape(new_len, kv_heads, group, HEAD_SIZE)
    key_head_rows = keys.astype(jnp.float32).reshape(total_len, kv_heads, HEAD_SIZE)
    value_head_rows = values.astype(jnp.float32).reshape(total_len, kv_heads, HEAD_SIZE)
    attention_scores = jnp.einsum('yfli,xfi->flyx', query_head_rows, key_head_rows) * HEAD_SIZE ** (-0.5)
    column = jnp.arange(total_len)[None, :]
    row_pos = jnp.arange(new_len)[:, None]
    visible = (column < step_len) | (column - step_len <= row_pos)
    attention_scores = jnp.where(visible, attention_scores, -jnp.inf)
    attention_weights = jax.nn.softmax(attention_scores, axis=-1).astype(jnp.bfloat16).astype(jnp.float32)
    attended_values = jnp.einsum('fjip,pfa->ifja', attention_weights, value_head_rows)
    return attended_values.reshape(new_len, -1).astype(jnp.bfloat16)

def reference(queries, new_keys, new_values, step_kv, prm_last, value_head, parents):
    hidden = prm_last.astype(jnp.float32)
    square = lax.optimization_barrier(jnp.mean(hidden * hidden, axis=-1, keepdims=True))
    normed = hidden * lax.rsqrt(square + 1e-05)
    score = jnp.dot(normed, value_head, precision=lax.Precision.HIGHEST)
    reward = jax.nn.sigmoid(score).astype(jnp.bfloat16)
    child_reward = jnp.take(reward, parents, axis=0).astype(jnp.float32)
    total = jnp.sum(child_reward)
    child_share = CHILDREN * child_reward / total
    copied = jnp.take(step_kv, parents, axis=0)
    keys_all = jnp.concatenate([copied[:, 0], new_keys], axis=1)
    values_all = jnp.concatenate([copied[:, 1], new_values], axis=1)
    attended = lax.map(attend_child, (queries, keys_all, values_all))
    return (attended, child_share)
```

```python
import functools

import jax
import jax.numpy as jnp
from jax import lax
from jax.experimental import pallas as pl
from jax.experimental.pallas import tpu as pltpu
from jax.sharding import PartitionSpec as P

HEAD_SIZE = 128
KEEP = 2
LOG2E = 1.4426950408889634


def remote(src, dst, send, recv, device):
    return pltpu.make_async_remote_copy(
        src_ref=src, dst_ref=dst, send_sem=send, recv_sem=recv,
        device_id={"beam": device}, device_id_type=pl.DeviceIdType.MESH,
    )


def loads(k, head, hbm, buf, isem):
    q_hbm, nk_hbm, nv_hbm = hbm
    qbuf, kbuf, vbuf, _ = buf
    width = qbuf.shape[3]
    half = q_hbm.shape[1] // 2
    cols = pl.ds(pl.multiple_of(head * HEAD_SIZE, HEAD_SIZE), HEAD_SIZE)
    wide = pl.ds(pl.multiple_of(head * width, width), width)
    lo, hi = pl.ds(0, half), pl.ds(half, half)
    return [
        pltpu.make_async_copy(q_hbm.at[:, :, wide], qbuf.at[k], isem.at[k, 0]),
        pltpu.make_async_copy(nk_hbm.at[:, hi, cols], kbuf.at[k, :, lo], isem.at[k, 1]),
        pltpu.make_async_copy(nk_hbm.at[:, lo, cols], kbuf.at[k, :, hi], isem.at[k, 2]),
        pltpu.make_async_copy(nv_hbm.at[:, hi, cols], vbuf.at[k, :, lo], isem.at[k, 3]),
        pltpu.make_async_copy(nv_hbm.at[:, lo, cols], vbuf.at[k, :, hi], isem.at[k, 4]),
    ]


def store(k, head, obuf, out_hbm, osem):
    width = obuf.shape[3]
    wide = pl.ds(pl.multiple_of(head * width, width), width)
    return pltpu.make_async_copy(obuf.at[k], out_hbm.at[:, :, wide], osem.at[k])


def attend(k, j, buf):
    qbuf, kbuf, vbuf, obuf = buf
    half = qbuf.shape[2] // 2
    group = qbuf.shape[3] // HEAD_SIZE
    row = lax.rem(lax.broadcasted_iota(jnp.int32, (group * half, half), 0), half)
    column = lax.broadcasted_iota(jnp.int32, (group * half, half), 1)
    visible = column <= row
    scale = HEAD_SIZE ** (-0.5) * LOG2E
    for part in range(2):
        start = half if part == 0 else 0
        keys = kbuf[k, j, start:]
        values = vbuf[k, j, start:]
        values = jnp.concatenate([values, jnp.ones_like(values)], axis=1)
        rows = slice(part * half, (part + 1) * half)
        query = jnp.concatenate(
            [qbuf[k, j, rows, g * HEAD_SIZE:(g + 1) * HEAD_SIZE] for g in range(group)],
            axis=0,
        )
        s = lax.dot_general(
            query, keys, (((1,), (1,)), ((), ())), preferred_element_type=jnp.float32
        )
        s = jnp.concatenate(
            [jnp.where(visible, s[:, :half], -jnp.inf), s[:, half:]], axis=1
        )
        top = jnp.max(s, axis=1, keepdims=True)
        p = jnp.exp2((s - top) * scale).astype(jnp.bfloat16)
        o = jnp.dot(p, values, preferred_element_type=jnp.float32)
        o = (o[:, :HEAD_SIZE] / o[:, HEAD_SIZE:]).astype(jnp.bfloat16)
        for g in range(group):
            obuf[k, j, rows, g * HEAD_SIZE:(g + 1) * HEAD_SIZE] = o[
                g * half:(g + 1) * half
            ]


def last_kernel(
    first, tail, part, q_hbm, nk_hbm, nv_hbm, out_hbm,
    qbuf, kbuf, vbuf, obuf, held, isem, osem, hin, hout,
):
    hbm = (q_hbm, nk_hbm, nv_hbm)
    buf = (qbuf, kbuf, vbuf, obuf)
    local, new_len, done = held.shape
    count = qbuf.shape[0]

    def fetch(j):
        return pltpu.make_async_copy(part.at[j], held.at[j], hin.at[j])

    def put(j):
        return pltpu.make_async_copy(
            held.at[j], out_hbm.at[j, :, pl.ds(0, done)], hout.at[j]
        )

    for k in range(count):
        for copy in loads(k, first + k, hbm, buf, isem):
            copy.start()
        if k == 0:
            for j in range(local):
                fetch(j).start()
    for k in range(count):
        for j in range(local):
            kbuf[k, j, new_len:] = tail[k, j, 0]
            vbuf[k, j, new_len:] = tail[k, j, 1]
    for k in range(count):
        for copy in loads(k, first + k, hbm, buf, isem):
            copy.wait()
        if k > 0:
            for j in range(local):
                fetch(j).wait()
                put(j).start()

        def one(j, carry):
            attend(k, j, buf)
            return carry

        lax.fori_loop(0, local, one, 0, unroll=2)
        store(k, first + k, obuf, out_hbm, osem).start()
    for j in range(local):
        put(j).wait()
    for k in range(count):
        store(k, first + k, obuf, out_hbm, osem).wait()


def kernel(
    n, ny, nz, idx, prm, head, kv, q_hbm, nk_hbm, nv_hbm, out_hbm, rbuf, tail,
    col, pbuf, ybuf, qbuf, kbuf, vbuf, obuf,
    rsend, rrecv, zsend, zrecv, lsend, csend, crecv, ysend, yrecv, isem, osem,
):
    me = lax.axis_index("beam")
    my_c = lax.rem(me, 2)
    my_y = lax.rem(lax.div(me, 2), ny)
    my_z = lax.div(me, 2 * ny)
    local = kv.shape[0]
    step_len = kv.shape[2]
    heads = kv.shape[3] // HEAD_SIZE
    new_len = q_hbm.shape[1]
    front = qbuf.shape[0]
    hbm = (q_hbm, nk_hbm, nv_hbm)
    buf = (qbuf, kbuf, vbuf, obuf)

    def at(z, y, c):
        return (z * ny + y) * 2 + c

    core_peer = at(my_z, my_y, 1 - my_c)
    y_peer = at(my_z, lax.rem(my_y + 1, ny), my_c)

    barrier = pltpu.get_barrier_semaphore()

    def greet(d, carry):
        pl.semaphore_signal(
            barrier, inc=1, device_id={"beam": lax.rem(me + d, n)},
            device_id_type=pl.DeviceIdType.MESH,
        )
        return carry

    lax.fori_loop(1, n, greet, 0)

    def load(k, carry):
        for copy in loads(k, k, hbm, buf, isem):
            copy.start()
        return carry

    lax.fori_loop(0, front, load, 0)

    for k in range(heads):
        cols = slice(k * HEAD_SIZE, (k + 1) * HEAD_SIZE)
        for r in range(KEEP):
            tile = kv[0, :, :, cols]
            for b in range(1, local):
                tile = jnp.where(idx[r] == b, kv[b, :, :, cols], tile)
            col[k, 0, my_z, r] = tile

    hidden = prm[...].astype(jnp.float32)
    square = jnp.mean(hidden * hidden, axis=-1, keepdims=True)
    normed = hidden * lax.rsqrt(square + 1e-05)
    score = jnp.sum(normed * head[...], axis=-1, keepdims=True)
    reward = (1.0 / (1.0 + jnp.exp(-score))).astype(jnp.bfloat16).astype(jnp.float32)
    rbuf[me] = jnp.broadcast_to(reward, (local, 128))

    pl.semaphore_wait(barrier, n - 1)

    def z_copy(k, d):
        zt = lax.rem(my_z + d, nz)
        return remote(
            col.at[k, 0, my_z], col.at[k, 0, my_z],
            zsend.at[k, d], zrecv.at[k, my_z], at(zt, my_y, my_c),
        )

    def z_arrival(k, d):
        zs = lax.rem(my_z + d, nz)
        return remote(
            col.at[k, 0, zs], col.at[k, 0, zs],
            zsend.at[k, d], zrecv.at[k, zs], at(zs, my_y, my_c),
        )

    relayed = nz == 4

    def when_direct(d, run):
        if relayed and d == 1:
            pl.when(my_z != nz - 1)(run)
        elif relayed and d == nz - 1:
            pl.when(my_z != 0)(run)
        else:
            run()

    def relay_copy(k, source, target):
        return remote(
            col.at[k, 0, source], col.at[k, 0, source],
            lsend.at[k], zrecv.at[k, source], at(target, my_y, my_c),
        )

    ends = ((nz - 2, 0, nz - 1), (1, nz - 1, 0)) if relayed else ()

    def relay(k):
        for who, source, target in ends:

            @pl.when(my_z == who)
            def _():
                relay_copy(k, source, target).wait_recv()
                relay_copy(k, source, target).start()

    def z_wait(k):
        for d in range(1, nz):
            zs = lax.rem(my_z + d, nz)
            got = (my_z == 1) & (zs == nz - 1) | (my_z == nz - 2) & (zs == 0)
            if relayed:

                @pl.when(jnp.logical_not(got))
                def _():
                    z_arrival(k, d).wait_recv()
            else:
                z_arrival(k, d).wait_recv()

    def z_start(k, carry):
        for d in range(1, nz):
            when_direct(d, z_copy(k, d).start)
        return carry

    def r_copy(d):
        return remote(rbuf.at[me], rbuf.at[me], rsend.at[d], rrecv.at[me], lax.rem(me + d, n))

    def r_arrival(d):
        src = lax.rem(me + d, n)
        return remote(rbuf.at[src], rbuf.at[src], rsend.at[d], rrecv.at[src], src)

    lax.fori_loop(0, heads, z_start, 0)

    def r_start(d, carry):
        r_copy(d).start()
        return carry

    lax.fori_loop(1, n, r_start, 0)

    def c_copy(k):
        return remote(col.at[k, 0], col.at[k, 1], csend.at[k], crecv.at[k], core_peer)

    def y_copy(k):
        return remote(pbuf.at[k], ybuf.at[k], ysend.at[k], yrecv.at[k], y_peer)

    def pick(k, codes, bases):
        tiles = list(bases)
        for c in range(2):
            for z in range(nz):
                for r in range(KEEP):
                    entry = col[k, c, z, r]
                    slot = (c * nz + z) * KEEP + r
                    tiles = [
                        jnp.where(code == slot, entry, tile)
                        for code, tile in zip(codes, tiles)
                    ]
        return tiles

    def exchange_one(k):
        z_wait(k)
        c_copy(k).start()

    def exchange_two(k):
        c_copy(k).wait_recv()
        if ny > 1:
            codes = [idx[KEEP + local + j] for j in range(local)]
            tiles = pick(k, codes, [col[k, 0, 0, 0]] * local)
            for j in range(local):
                pbuf[k, j] = tiles[j]
            y_copy(k).start()

    def parents_of(k):
        if ny > 1:
            y_copy(k).wait_recv()
        bases = [ybuf[k, j] if ny > 1 else col[k, 0, 0, 0] for j in range(local)]
        return pick(k, [idx[KEEP + j] for j in range(local)], bases)

    def place(k):
        tiles = parents_of(k)
        for j in range(local):
            kbuf[k, j, new_len:] = tiles[j][0]
            vbuf[k, j, new_len:] = tiles[j][1]

    def attend_some(k, first, last):
        def one(j, carry):
            attend(k, j, buf)
            return carry

        lax.fori_loop(first, last, one, 0, unroll=True)

    def ready(k):
        for copy in loads(k, k, hbm, buf, isem):
            copy.wait()
        place(k)

    def finish_head(k):
        attend_some(k, local // 2, local)
        store(k, k, obuf, out_hbm, osem).start()

    def start_head(k):
        ready(k)
        attend_some(k, 0, local // 2)

    relay(0)
    exchange_one(0)
    relay(1)
    exchange_one(1)
    exchange_two(0)
    relay(2)

    def step(k, carry):
        exchange_one(k)
        exchange_two(k - 1)
        pl.when(k + 1 < heads)(functools.partial(relay, k + 1))
        start_head(k - 2)
        finish_head(k - 2)
        return carry

    lax.fori_loop(2, heads, step, 0)
    exchange_two(heads - 1)
    for k in range(front, heads):
        tiles = parents_of(k)
        for j in range(local):
            tail[k - front, j] = tiles[j]

    def finish(k, carry):
        for d in range(1, nz):
            when_direct(d, z_copy(k, d).wait_send)
        for who, source, target in ends:
            pl.when(my_z == who)(relay_copy(k, source, target).wait_send)
        c_copy(k).wait_send()
        if ny > 1:
            y_copy(k).wait_send()
        return carry

    lax.fori_loop(0, heads, finish, 0)

    def stored(k, carry):
        store(k, k, obuf, out_hbm, osem).wait()
        return carry

    lax.fori_loop(0, front, stored, 0)

    def r_finish(d, carry):
        r_arrival(d).wait_recv()
        r_copy(d).wait_send()
        return carry

    lax.fori_loop(1, n, r_finish, 0)


def plane_kernel(
    nz, idx, prm, head, kv, q_hbm, nk_hbm, nv_hbm, out_hbm, rbuf, tail, *scratch
):
    local, _, step_len, kv_width = kv.shape
    heads = kv_width // HEAD_SIZE
    raws = scratch[:heads]
    (
        kept, picked, share, held, qbuf, kbuf, vbuf, obuf,
        rsend, rrecv, asend, arecv, zsend, zrecv, psend, precv,
        msend, mrecv, isem, osem,
    ) = scratch[heads:]
    me = lax.axis_index("beam")
    plane = kept.shape[1]
    n = nz * plane
    rows = step_len // plane
    new_len = q_hbm.shape[1]
    front = qbuf.shape[0]
    hbm = (q_hbm, nk_hbm, nv_hbm)
    buf = (qbuf, kbuf, vbuf, obuf)
    my_q = lax.rem(me, plane)
    my_z = lax.div(me, plane)
    inner = (my_z == 1) | (my_z == 2)
    outer = jnp.logical_not(inner)
    near = jnp.where(my_z < 2, 1 - my_z, 5 - my_z)
    my_rows = pl.ds(pl.multiple_of(my_q * rows, rows), rows)

    barrier = pltpu.get_barrier_semaphore()

    def greet(d, carry):
        pl.semaphore_signal(
            barrier, inc=1, device_id={"beam": lax.rem(me + d, n)},
            device_id_type=pl.DeviceIdType.MESH,
        )
        return carry

    lax.fori_loop(1, n, greet, 0)

    for k in range(heads):
        cols = slice(k * HEAD_SIZE, (k + 1) * HEAD_SIZE)
        for r in range(KEEP):
            for q in range(plane):
                kept[k, q, r] = kv[idx[r], :, q * rows:(q + 1) * rows, cols]
            raws[k][me * KEEP + r] = kv[idx[r], :, my_rows, cols]

    pl.semaphore_wait(barrier, n - 1)

    def mate(d):
        return lax.rem(my_q + d, plane)

    def a_copy(k, d):
        q = mate(d)
        slot = pl.ds(me * KEEP, KEEP)
        return remote(
            kept.at[k, q], raws[k].at[slot], asend.at[k, d], arecv.at[k, my_q],
            my_z * plane + q,
        )

    def a_arrival(k, d):
        q = mate(d)
        slot = pl.ds((my_z * plane + q) * KEEP, KEEP)
        return remote(
            kept.at[k, q], raws[k].at[slot], asend.at[k, d], arecv.at[k, q],
            my_z * plane + q,
        )

    def z_copy(k, i, target):
        slot = pl.ds(my_z * plane * KEEP, plane * KEEP)
        return remote(
            raws[k].at[slot], raws[k].at[slot], zsend.at[k, i], zrecv.at[k, my_z],
            target * plane + my_q,
        )

    def z_arrival(k, d):
        z = lax.rem(my_z + d, nz)
        slot = pl.ds(z * plane * KEEP, plane * KEEP)
        return remote(
            raws[k].at[slot], raws[k].at[slot], zsend.at[k, 0], zrecv.at[k, z],
            z * plane + my_q,
        )

    def p_copy(k):
        return remote(
            picked.at[k], share.at[k], psend.at[k], precv.at[k], near * plane + my_q
        )

    def m_copy(k, d):
        q = mate(d)
        return remote(
            share.at[k, pl.ds(q * local, local)], held.at[k, :, :, my_rows],
            msend.at[k, d], mrecv.at[k, my_q], my_z * plane + q,
        )

    def m_arrival(k, d):
        q = mate(d)
        theirs = pl.ds(pl.multiple_of(q * rows, rows), rows)
        return remote(
            share.at[k, pl.ds(q * local, local)], held.at[k, :, :, theirs],
            msend.at[k, d], mrecv.at[k, q], my_z * plane + q,
        )

    def r_copy(d):
        return remote(rbuf.at[me], rbuf.at[me], rsend.at[d], rrecv.at[me], lax.rem(me + d, n))

    def r_arrival(d):
        src = lax.rem(me + d, n)
        return remote(rbuf.at[src], rbuf.at[src], rsend.at[d], rrecv.at[src], src)

    for k in range(heads):
        for d in range(1, plane):
            a_copy(k, d).start()

    def load(k, carry):
        for copy in loads(k, k, hbm, buf, isem):
            copy.start()
        return carry

    lax.fori_loop(0, front, load, 0)

    for k in range(heads):
        for d in range(1, plane):
            a_arrival(k, d).wait_recv()

        @pl.when(outer)
        def _():
            z_copy(k, 0, nz - 1 - near).start()
            z_copy(k, 1, near).start()

        @pl.when(inner)
        def _():
            z_copy(k, 0, nz - 1 - my_z).start()

    hidden = prm[...].astype(jnp.float32)
    square = jnp.mean(hidden * hidden, axis=-1, keepdims=True)
    normed = hidden * lax.rsqrt(square + 1e-05)
    score = jnp.sum(normed * head[...], axis=-1, keepdims=True)
    reward = (1.0 / (1.0 + jnp.exp(-score))).astype(jnp.bfloat16).astype(jnp.float32)
    rbuf[me] = jnp.broadcast_to(reward, (local, 128))

    def r_start(d, carry):
        r_copy(d).start()
        return carry

    lax.fori_loop(1, n, r_start, 0)

    def pass_on(k):
        @pl.when(inner)
        def _():
            for d in range(1, nz):
                z_arrival(k, d).wait_recv()
            for t in range(plane * local):
                picked[k, t] = raws[k][idx[KEEP + near * plane * local + t]]
            p_copy(k).start()
            for t in range(plane * local):
                share[k, t] = raws[k][idx[KEEP + my_z * plane * local + t]]

        @pl.when(outer)
        def _():
            p_copy(k).wait_recv()

        for d in range(1, plane):
            m_copy(k, d).start()
        held[k, :, :, my_rows] = share[k, pl.ds(my_q * local, local)]

    def arrived(k):
        for d in range(1, plane):
            m_arrival(k, d).wait_recv()

    def ready(k):
        for copy in loads(k, k, hbm, buf, isem):
            copy.wait()
        arrived(k)
        for j in range(local):
            kbuf[k, j, new_len:] = held[k, j, 0]
            vbuf[k, j, new_len:] = held[k, j, 1]

    pass_on(0)

    def step(k, carry):
        for later in range(1, heads):
            pl.when(k + 1 == later)(functools.partial(pass_on, later))

        @pl.when(k < front)
        def _():
            ready(k)

            def one(j, inside):
                attend(k, j, buf)
                return inside

            lax.fori_loop(0, local, one, 0, unroll=True)
            store(k, k, obuf, out_hbm, osem).start()
        return carry

    lax.fori_loop(0, heads - 1, step, 0)
    for k in range(front, heads):
        arrived(k)
        for j in range(local):
            tail[k - front, j] = held[k, j]

    for k in range(heads):
        for d in range(1, plane):
            a_copy(k, d).wait_send()
            m_copy(k, d).wait_send()

        @pl.when(outer)
        def _():
            z_copy(k, 0, nz - 1 - near).wait_send()
            z_copy(k, 1, near).wait_send()

        @pl.when(inner)
        def _():
            z_copy(k, 0, nz - 1 - my_z).wait_send()
            p_copy(k).wait_send()

    def stored(k, carry):
        store(k, k, obuf, out_hbm, osem).wait()
        return carry

    lax.fori_loop(0, front, stored, 0)

    def r_finish(d, carry):
        r_arrival(d).wait_recv()
        r_copy(d).wait_send()
        return carry

    lax.fori_loop(1, n, r_finish, 0)


def body(queries, new_keys, new_values, step_kv, prm_last, value_head, parents):
    n = lax.axis_size("beam")
    ny = 2 if n == 16 else 1
    nz = n // (2 * ny)
    me = lax.axis_index("beam")
    local, new_len, qwidth = queries.shape
    children = parents.shape[0]
    step_len, kv_width = step_kv.shape[2:]
    heads = kv_width // HEAD_SIZE
    width = qwidth // heads

    beams = jnp.arange(n * local, dtype=jnp.int32)
    equal = parents[None, :] == beams[:, None]
    hits = jnp.sum(equal.astype(jnp.int32), axis=1)
    kept = (hits > 0).astype(jnp.int32)
    before = jnp.sum(kept[None, :] * (beams[None, :] < beams[:, None]), axis=1)
    rank_of_beam = before % KEEP
    wanted = (
        (beams[None, :] // local == me)
        & (kept[None, :] > 0)
        & (rank_of_beam[None, :] == jnp.arange(KEEP, dtype=jnp.int32)[:, None])
    )
    keep_pos = jnp.sum(wanted * (beams % local)[None, :], axis=1).astype(jnp.int32)
    rank = jnp.sum(equal * rank_of_beam[:, None], axis=0)
    owner = parents // local
    c, y, z = owner % 2, (owner // 2) % ny, owner // (2 * ny)
    my_c, my_y = me % 2, (me // 2) % ny
    code = jnp.where(y == my_y, ((c != my_c) * nz + z) * KEEP + rank, -1).astype(jnp.int32)
    y_peer = me + 2 - 4 * my_y if ny > 1 else me
    own = lax.dynamic_slice_in_dim(code, me * local, local)
    other = lax.dynamic_slice_in_dim(code, y_peer * local, local)
    idx = jnp.concatenate([keep_pos, own, other])

    dma = pltpu.SemaphoreType.DMA
    bf16 = jnp.bfloat16
    vmem = pl.BlockSpec(memory_space=pltpu.VMEM)
    anywhere = pl.BlockSpec(memory_space=pl.ANY)
    last = 2
    front = heads - last
    dma_pair = lambda *shape: [dma(shape), dma(shape)]
    blocks = [
        pltpu.VMEM((front, local, new_len, width), bf16),
        pltpu.VMEM((front, local, new_len + step_len, HEAD_SIZE), bf16),
        pltpu.VMEM((front, local, new_len + step_len, HEAD_SIZE), bf16),
        pltpu.VMEM((front, local, new_len, width), bf16),
    ]
    ends = [dma((front, 5)), dma((front,))]
    planes = ny == 2 and nz == 4
    if planes:
        plane = 2 * ny
        rows = step_len // plane
        run = functools.partial(plane_kernel, nz)
        scratch = (
            [pltpu.VMEM((n * KEEP, 2, rows, HEAD_SIZE), bf16)] * heads
            + [
                pltpu.VMEM((heads, plane, KEEP, 2, rows, HEAD_SIZE), bf16),
                pltpu.VMEM((heads, plane * local, 2, rows, HEAD_SIZE), bf16),
                pltpu.VMEM((heads, plane * local, 2, rows, HEAD_SIZE), bf16),
                pltpu.VMEM((heads, local, 2, step_len, HEAD_SIZE), bf16),
            ]
            + blocks + dma_pair(n) + dma_pair(heads, plane)
            + [dma((heads, 2)), dma((heads, nz))] + dma_pair(heads)
            + dma_pair(heads, plane) + ends
        )
        idx = jnp.concatenate([keep_pos, owner * KEEP + rank]).astype(jnp.int32)
    else:
        run = functools.partial(kernel, n, ny, nz)
        scratch = (
            [
                pltpu.VMEM((heads, 2, nz, KEEP, 2, step_len, HEAD_SIZE), bf16),
                pltpu.VMEM((heads, local, 2, step_len, HEAD_SIZE), bf16),
                pltpu.VMEM((heads, local, 2, step_len, HEAD_SIZE), bf16),
            ]
            + blocks + dma_pair(n) + dma_pair(heads, nz) + [dma((heads,))]
            + dma_pair(heads) + dma_pair(heads) + ends
        )
    part, rewards, tail = pl.pallas_call(
        run,
        out_shape=(
            jax.ShapeDtypeStruct((local, new_len, front * width), bf16),
            jax.ShapeDtypeStruct((n, local, 128), jnp.float32),
            jax.ShapeDtypeStruct((last, local, 2, step_len, HEAD_SIZE), bf16),
        ),
        in_specs=[pl.BlockSpec(memory_space=pltpu.SMEM), vmem, vmem, vmem]
        + [anywhere] * 3,
        out_specs=(anywhere, vmem, vmem),
        scratch_shapes=scratch,
        compiler_params=pltpu.CompilerParams(
            collective_id=0, has_side_effects=True, vmem_limit_bytes=56 << 20
        ),
    )(idx, prm_last, value_head.reshape(1, -1), step_kv, queries, new_keys, new_values)

    attended = pl.pallas_call(
        functools.partial(last_kernel, front),
        out_shape=jax.ShapeDtypeStruct(queries.shape, bf16),
        in_specs=[vmem] + [anywhere] * 4,
        out_specs=anywhere,
        scratch_shapes=[
            pltpu.VMEM((last, local, new_len, width), bf16),
            pltpu.VMEM((last, local, new_len + step_len, HEAD_SIZE), bf16),
            pltpu.VMEM((last, local, new_len + step_len, HEAD_SIZE), bf16),
            pltpu.VMEM((last, local, new_len, width), bf16),
            pltpu.VMEM((local, new_len, front * width), bf16),
            dma((last, 5)), dma((last,)), dma((local,)), dma((local,)),
        ],
        compiler_params=pltpu.CompilerParams(vmem_limit_bytes=56 << 20),
    )(tail, part, queries, new_keys, new_values)

    reward = rewards[:, :, 0].reshape(-1)
    total = jnp.sum(reward * hits.astype(jnp.float32))
    mine = lax.dynamic_slice_in_dim(parents, me * local, local)
    match = mine[:, None] == beams[None, :]
    child_reward = jnp.sum(jnp.where(match, reward[None, :], 0.0), axis=1)
    child_share = children * child_reward / total
    return (attended, child_share)


def solution(mesh):
    in_specs = (
        P(("prompts", "beam"), None, None),
        P(("prompts", "beam"), None, None),
        P(("prompts", "beam"), None, None),
        P(("prompts", "beam"), None, None, None),
        P(("prompts", "beam"), None),
        P(),
        P("prompts"),
    )
    out_specs = (P(("prompts", "beam"), None, None), P(("prompts", "beam")))
    return jax.shard_map(body, mesh=mesh, in_specs=in_specs, out_specs=out_specs, check_vma=False)
```

```python
import functools

import jax
import jax.numpy as jnp
from jax import lax
from jax.experimental import pallas as pl
from jax.experimental.pallas import tpu as pltpu
from jax.sharding import PartitionSpec as P

HEAD_SIZE = 128
KEEP = 2
LOG2E = 1.4426950408889634


def remote(src, dst, send, recv, device):
    return pltpu.make_async_remote_copy(
        src_ref=src, dst_ref=dst, send_sem=send, recv_sem=recv,
        device_id={"beam": device}, device_id_type=pl.DeviceIdType.MESH,
    )


def loads(k, head, hbm, buf, isem):
    q_hbm, nk_hbm, nv_hbm = hbm
    qbuf, kbuf, vbuf, _ = buf
    width = qbuf.shape[3]
    half = q_hbm.shape[1] // 2
    cols = pl.ds(pl.multiple_of(head * HEAD_SIZE, HEAD_SIZE), HEAD_SIZE)
    wide = pl.ds(pl.multiple_of(head * width, width), width)
    lo, hi = pl.ds(0, half), pl.ds(half, half)
    return [
        pltpu.make_async_copy(q_hbm.at[:, :, wide], qbuf.at[k], isem.at[k, 0]),
        pltpu.make_async_copy(nk_hbm.at[:, hi, cols], kbuf.at[k, :, lo], isem.at[k, 1]),
        pltpu.make_async_copy(nk_hbm.at[:, lo, cols], kbuf.at[k, :, hi], isem.at[k, 2]),
        pltpu.make_async_copy(nv_hbm.at[:, hi, cols], vbuf.at[k, :, lo], isem.at[k, 3]),
        pltpu.make_async_copy(nv_hbm.at[:, lo, cols], vbuf.at[k, :, hi], isem.at[k, 4]),
    ]


def store(k, head, obuf, out_hbm, osem):
    width = obuf.shape[3]
    wide = pl.ds(pl.multiple_of(head * width, width), width)
    return pltpu.make_async_copy(obuf.at[k], out_hbm.at[:, :, wide], osem.at[k])


def attend(k, j, buf):
    qbuf, kbuf, vbuf, obuf = buf
    half = qbuf.shape[2] // 2
    group = qbuf.shape[3] // HEAD_SIZE
    row = lax.rem(lax.broadcasted_iota(jnp.int32, (group * half, half), 0), half)
    column = lax.broadcasted_iota(jnp.int32, (group * half, half), 1)
    visible = column <= row
    scale = HEAD_SIZE ** (-0.5) * LOG2E
    for part in range(2):
        start = half if part == 0 else 0
        keys = kbuf[k, j, start:]
        values = vbuf[k, j, start:]
        values = jnp.concatenate([values, jnp.ones_like(values)], axis=1)
        rows = slice(part * half, (part + 1) * half)
        query = jnp.concatenate(
            [qbuf[k, j, rows, g * HEAD_SIZE:(g + 1) * HEAD_SIZE] for g in range(group)],
            axis=0,
        )
        s = lax.dot_general(
            query, keys, (((1,), (1,)), ((), ())), preferred_element_type=jnp.float32
        )
        s = jnp.concatenate(
            [jnp.where(visible, s[:, :half], -jnp.inf), s[:, half:]], axis=1
        )
        top = jnp.max(s, axis=1, keepdims=True)
        p = jnp.exp2((s - top) * scale).astype(jnp.bfloat16)
        o = jnp.dot(p, values, preferred_element_type=jnp.float32)
        o = (o[:, :HEAD_SIZE] / o[:, HEAD_SIZE:]).astype(jnp.bfloat16)
        for g in range(group):
            obuf[k, j, rows, g * HEAD_SIZE:(g + 1) * HEAD_SIZE] = o[
                g * half:(g + 1) * half
            ]


def last_kernel(
    first, tail, part, q_hbm, nk_hbm, nv_hbm, out_hbm,
    qbuf, kbuf, vbuf, obuf, held, isem, osem, hin, hout,
):
    hbm = (q_hbm, nk_hbm, nv_hbm)
    buf = (qbuf, kbuf, vbuf, obuf)
    local, new_len, done = held.shape
    count = qbuf.shape[0]

    def fetch(j):
        return pltpu.make_async_copy(part.at[j], held.at[j], hin.at[j])

    def put(j):
        return pltpu.make_async_copy(
            held.at[j], out_hbm.at[j, :, pl.ds(0, done)], hout.at[j]
        )

    for k in range(count):
        for copy in loads(k, first + k, hbm, buf, isem):
            copy.start()
        if k == 0:
            for j in range(local):
                fetch(j).start()
    for k in range(count):
        for j in range(local):
            kbuf[k, j, new_len:] = tail[k, j, 0]
            vbuf[k, j, new_len:] = tail[k, j, 1]
    for k in range(count):
        for copy in loads(k, first + k, hbm, buf, isem):
            copy.wait()
        if k > 0:
            for j in range(local):
                fetch(j).wait()
                put(j).start()

        def one(j, carry):
            attend(k, j, buf)
            return carry

        lax.fori_loop(0, local, one, 0, unroll=2)
        store(k, first + k, obuf, out_hbm, osem).start()
    for j in range(local):
        put(j).wait()
    for k in range(count):
        store(k, first + k, obuf, out_hbm, osem).wait()


def kernel(
    n, ny, nz, idx, prm, head, kv, q_hbm, nk_hbm, nv_hbm, out_hbm, rbuf, tail,
    col, pbuf, ybuf, qbuf, kbuf, vbuf, obuf,
    rsend, rrecv, zsend, zrecv, lsend, csend, crecv, ysend, yrecv, isem, osem,
):
    me = lax.axis_index("beam")
    my_c = lax.rem(me, 2)
    my_y = lax.rem(lax.div(me, 2), ny)
    my_z = lax.div(me, 2 * ny)
    local = kv.shape[0]
    step_len = kv.shape[2]
    heads = kv.shape[3] // HEAD_SIZE
    new_len = q_hbm.shape[1]
    front = qbuf.shape[0]
    hbm = (q_hbm, nk_hbm, nv_hbm)
    buf = (qbuf, kbuf, vbuf, obuf)

    def at(z, y, c):
        return (z * ny + y) * 2 + c

    core_peer = at(my_z, my_y, 1 - my_c)
    y_peer = at(my_z, lax.rem(my_y + 1, ny), my_c)

    barrier = pltpu.get_barrier_semaphore()

    def greet(d, carry):
        pl.semaphore_signal(
            barrier, inc=1, device_id={"beam": lax.rem(me + d, n)},
            device_id_type=pl.DeviceIdType.MESH,
        )
        return carry

    lax.fori_loop(1, n, greet, 0)

    def load(k, carry):
        for copy in loads(k, k, hbm, buf, isem):
            copy.start()
        return carry

    lax.fori_loop(0, front, load, 0)

    for k in range(heads):
        cols = slice(k * HEAD_SIZE, (k + 1) * HEAD_SIZE)
        for r in range(KEEP):
            tile = kv[0, :, :, cols]
            for b in range(1, local):
                tile = jnp.where(idx[r] == b, kv[b, :, :, cols], tile)
            col[k, 0, my_z, r] = tile

    hidden = prm[...].astype(jnp.float32)
    square = jnp.mean(hidden * hidden, axis=-1, keepdims=True)
    normed = hidden * lax.rsqrt(square + 1e-05)
    score = jnp.sum(normed * head[...], axis=-1, keepdims=True)
    reward = (1.0 / (1.0 + jnp.exp(-score))).astype(jnp.bfloat16).astype(jnp.float32)
    rbuf[me] = jnp.broadcast_to(reward, (local, 128))

    pl.semaphore_wait(barrier, n - 1)

    def z_copy(k, d):
        zt = lax.rem(my_z + d, nz)
        return remote(
            col.at[k, 0, my_z], col.at[k, 0, my_z],
            zsend.at[k, d], zrecv.at[k, my_z], at(zt, my_y, my_c),
        )

    def z_arrival(k, d):
        zs = lax.rem(my_z + d, nz)
        return remote(
            col.at[k, 0, zs], col.at[k, 0, zs],
            zsend.at[k, d], zrecv.at[k, zs], at(zs, my_y, my_c),
        )

    relayed = nz == 4

    def when_direct(d, run):
        if relayed and d == 1:
            pl.when(my_z != nz - 1)(run)
        elif relayed and d == nz - 1:
            pl.when(my_z != 0)(run)
        else:
            run()

    def relay_copy(k, source, target):
        return remote(
            col.at[k, 0, source], col.at[k, 0, source],
            lsend.at[k], zrecv.at[k, source], at(target, my_y, my_c),
        )

    ends = ((nz - 2, 0, nz - 1), (1, nz - 1, 0)) if relayed else ()

    def relay(k):
        for who, source, target in ends:

            @pl.when(my_z == who)
            def _():
                relay_copy(k, source, target).wait_recv()
                relay_copy(k, source, target).start()

    def z_wait(k):
        for d in range(1, nz):
            zs = lax.rem(my_z + d, nz)
            got = (my_z == 1) & (zs == nz - 1) | (my_z == nz - 2) & (zs == 0)
            if relayed:

                @pl.when(jnp.logical_not(got))
                def _():
                    z_arrival(k, d).wait_recv()
            else:
                z_arrival(k, d).wait_recv()

    def z_start(k, carry):
        for d in range(1, nz):
            when_direct(d, z_copy(k, d).start)
        return carry

    def r_copy(d):
        return remote(rbuf.at[me], rbuf.at[me], rsend.at[d], rrecv.at[me], lax.rem(me + d, n))

    def r_arrival(d):
        src = lax.rem(me + d, n)
        return remote(rbuf.at[src], rbuf.at[src], rsend.at[d], rrecv.at[src], src)

    lax.fori_loop(0, heads, z_start, 0)

    def r_start(d, carry):
        r_copy(d).start()
        return carry

    lax.fori_loop(1, n, r_start, 0)

    def c_copy(k):
        return remote(col.at[k, 0], col.at[k, 1], csend.at[k], crecv.at[k], core_peer)

    def y_copy(k):
        return remote(pbuf.at[k], ybuf.at[k], ysend.at[k], yrecv.at[k], y_peer)

    def pick(k, codes, bases):
        tiles = list(bases)
        for c in range(2):
            for z in range(nz):
                for r in range(KEEP):
                    entry = col[k, c, z, r]
                    slot = (c * nz + z) * KEEP + r
                    tiles = [
                        jnp.where(code == slot, entry, tile)
                        for code, tile in zip(codes, tiles)
                    ]
        return tiles

    def exchange_one(k):
        z_wait(k)
        c_copy(k).start()

    def exchange_two(k):
        c_copy(k).wait_recv()
        if ny > 1:
            codes = [idx[KEEP + local + j] for j in range(local)]
            tiles = pick(k, codes, [col[k, 0, 0, 0]] * local)
            for j in range(local):
                pbuf[k, j] = tiles[j]
            y_copy(k).start()

    def parents_of(k):
        if ny > 1:
            y_copy(k).wait_recv()
        bases = [ybuf[k, j] if ny > 1 else col[k, 0, 0, 0] for j in range(local)]
        return pick(k, [idx[KEEP + j] for j in range(local)], bases)

    def place(k):
        tiles = parents_of(k)
        for j in range(local):
            kbuf[k, j, new_len:] = tiles[j][0]
            vbuf[k, j, new_len:] = tiles[j][1]

    def attend_some(k, first, last):
        def one(j, carry):
            attend(k, j, buf)
            return carry

        lax.fori_loop(first, last, one, 0, unroll=True)

    def ready(k):
        for copy in loads(k, k, hbm, buf, isem):
            copy.wait()
        place(k)

    def finish_head(k):
        attend_some(k, local // 2, local)
        store(k, k, obuf, out_hbm, osem).start()

    def start_head(k):
        ready(k)
        attend_some(k, 0, local // 2)

    relay(0)
    exchange_one(0)
    relay(1)
    exchange_one(1)
    exchange_two(0)
    relay(2)

    def step(k, carry):
        exchange_one(k)
        exchange_two(k - 1)
        pl.when(k + 1 < heads)(functools.partial(relay, k + 1))
        start_head(k - 2)
        finish_head(k - 2)
        return carry

    lax.fori_loop(2, heads, step, 0)
    exchange_two(heads - 1)
    for k in range(front, heads):
        tiles = parents_of(k)
        for j in range(local):
            tail[k - front, j] = tiles[j]

    def finish(k, carry):
        for d in range(1, nz):
            when_direct(d, z_copy(k, d).wait_send)
        for who, source, target in ends:
            pl.when(my_z == who)(relay_copy(k, source, target).wait_send)
        c_copy(k).wait_send()
        if ny > 1:
            y_copy(k).wait_send()
        return carry

    lax.fori_loop(0, heads, finish, 0)

    def stored(k, carry):
        store(k, k, obuf, out_hbm, osem).wait()
        return carry

    lax.fori_loop(0, front, stored, 0)

    def r_finish(d, carry):
        r_arrival(d).wait_recv()
        r_copy(d).wait_send()
        return carry

    lax.fori_loop(1, n, r_finish, 0)


def halves(heads):
    return [(k, 0, 2) for k in range(heads - 1)] + [(heads - 1, 0, 1), (heads - 1, 1, 1)]


def plane_kernel(
    nz, listed, parents, prm, head, kv, q_hbm, nk_hbm, nv_hbm,
    obuf, rbuf, qlast, klast, vlast, *scratch
):
    local, _, step_len, kv_width = kv.shape
    heads = kv_width // HEAD_SIZE
    chunks = halves(heads)
    raws = scratch[:len(chunks)]
    (
        kept, picked, share, held, qbuf, kbuf, vbuf, crow, code,
        rsend, rrecv, asend, arecv, zsend, zrecv, psend, precv,
        msend, mrecv, isem, csem,
    ) = scratch[len(chunks):]
    me = lax.axis_index("beam")
    plane = kept.shape[1]
    n = nz * plane
    rows = step_len // plane
    new_len = q_hbm.shape[1]
    front = qbuf.shape[0]
    hbm = (q_hbm, nk_hbm, nv_hbm)
    buf = (qbuf, kbuf, vbuf, obuf)
    my_q = lax.rem(me, plane)
    my_z = lax.div(me, plane)
    inner = (my_z == 1) | (my_z == 2)
    outer = jnp.logical_not(inner)
    near = jnp.where(my_z < 2, 1 - my_z, 5 - my_z)
    my_rows = pl.ds(pl.multiple_of(my_q * rows, rows), rows)

    barrier = pltpu.get_barrier_semaphore()

    def greet(d, carry):
        pl.semaphore_signal(
            barrier, inc=1, device_id={"beam": lax.rem(me + d, n)},
            device_id_type=pl.DeviceIdType.MESH,
        )
        return carry

    lax.fori_loop(1, n, greet, 0)

    low, high = local - 1, 0
    for c in range(listed.shape[0]):
        place = listed[c] - me * local
        mine = (place >= 0) & (place < local)
        low = jnp.where(mine, jnp.minimum(low, place), low)
        high = jnp.where(mine, jnp.maximum(high, place), high)
    for c, (k, lo, count) in enumerate(chunks):
        cols = slice(k * HEAD_SIZE, (k + 1) * HEAD_SIZE)
        part = slice(lo, lo + count)
        for r, beam in enumerate((low, high)):
            for q in range(plane):
                kept[k, q, r, part] = kv[beam, part, q * rows:(q + 1) * rows, cols]
            raws[c][me * KEEP + r] = kv[beam, part, my_rows, cols]

    pl.semaphore_wait(barrier, n - 1)

    def mate(d):
        return lax.rem(my_q + d, plane)

    def a_part(c, q, source):
        k, lo, count = chunks[c]
        slot = pl.ds((my_z * plane + source) * KEEP, KEEP)
        return kept.at[k, q, :, pl.ds(lo, count)], raws[c].at[slot]

    def a_copy(c, d):
        src, dst = a_part(c, mate(d), my_q)
        return remote(
            src, dst, asend.at[c, d], arecv.at[c, my_q], my_z * plane + mate(d)
        )

    def a_arrival(c, d):
        src, dst = a_part(c, mate(d), mate(d))
        return remote(
            src, dst, asend.at[c, d], arecv.at[c, mate(d)], my_z * plane + mate(d)
        )

    def z_copy(c, i, target):
        slot = pl.ds(my_z * plane * KEEP, plane * KEEP)
        return remote(
            raws[c].at[slot], raws[c].at[slot], zsend.at[c, i], zrecv.at[c, my_z],
            target * plane + my_q,
        )

    def z_arrival(c, d):
        z = lax.rem(my_z + d, nz)
        slot = pl.ds(z * plane * KEEP, plane * KEEP)
        return remote(
            raws[c].at[slot], raws[c].at[slot], zsend.at[c, 0], zrecv.at[c, z],
            z * plane + my_q,
        )

    def p_copy(c):
        k, lo, count = chunks[c]
        part = pl.ds(lo, count)
        return remote(
            picked.at[k, :, part], share.at[k, :, part], psend.at[c], precv.at[c],
            near * plane + my_q,
        )

    def m_part(c, q, source):
        k, lo, count = chunks[c]
        part = pl.ds(lo, count)
        theirs = pl.ds(pl.multiple_of(source * rows, rows), rows)
        return (
            share.at[k, pl.ds(q * local, local), part],
            held.at[k, :, part, theirs],
        )

    def m_copy(c, d):
        src, dst = m_part(c, mate(d), my_q)
        return remote(
            src, dst, msend.at[c, d], mrecv.at[c, my_q], my_z * plane + mate(d)
        )

    def m_arrival(c, d):
        src, dst = m_part(c, mate(d), mate(d))
        return remote(
            src, dst, msend.at[c, d], mrecv.at[c, mate(d)], my_z * plane + mate(d)
        )

    def r_copy(d):
        return remote(rbuf.at[me], rbuf.at[me], rsend.at[d], rrecv.at[me], lax.rem(me + d, n))

    def r_arrival(d):
        src = lax.rem(me + d, n)
        return remote(rbuf.at[src], rbuf.at[src], rsend.at[d], rrecv.at[src], src)

    for c in range(len(chunks)):
        for d in range(1, plane):
            a_copy(c, d).start()

    ids = parents[...]
    owner = lax.div(ids, local)
    groups = lax.broadcasted_iota(jnp.int32, (n, ids.shape[1]), 0)
    own = groups == owner
    first = jnp.min(jnp.where(own, ids, n * local), axis=1, keepdims=True)
    first = jnp.min(jnp.where(own, first, n * local), axis=0, keepdims=True)
    crow[...] = owner * KEEP + (ids > first).astype(jnp.int32)
    numbers = pltpu.make_async_copy(crow, code, csem)
    numbers.start()

    def last_loads():
        return loads(0, heads - 1, hbm, (qlast, klast, vlast, None), isem.at[pl.ds(front, 1)])

    def load(k, carry):
        for copy in loads(k, k, hbm, buf, isem):
            copy.start()
        return carry

    lax.fori_loop(0, front, load, 0)
    for copy in last_loads():
        copy.start()

    for c in range(len(chunks)):
        for d in range(1, plane):
            a_arrival(c, d).wait_recv()

        @pl.when(outer)
        def _():
            z_copy(c, 0, nz - 1 - near).start()
            z_copy(c, 1, near).start()

        @pl.when(inner)
        def _():
            z_copy(c, 0, nz - 1 - my_z).start()

    hidden = prm[...].astype(jnp.float32)
    square = jnp.mean(hidden * hidden, axis=-1, keepdims=True)
    normed = hidden * lax.rsqrt(square + 1e-05)
    score = jnp.sum(normed * head[...], axis=-1, keepdims=True)
    reward = (1.0 / (1.0 + jnp.exp(-score))).astype(jnp.bfloat16).astype(jnp.float32)
    rbuf[me] = jnp.broadcast_to(reward, (local, 128))

    def r_start(d, carry):
        r_copy(d).start()
        return carry

    lax.fori_loop(1, n, r_start, 0)
    numbers.wait()

    def pass_on(c):
        k, lo, count = chunks[c]
        part = slice(lo, lo + count)

        @pl.when(inner)
        def _():
            for d in range(1, nz):
                z_arrival(c, d).wait_recv()
            for t in range(plane * local):
                picked[k, t, part] = raws[c][code[0, near * plane * local + t]]
            p_copy(c).start()
            for t in range(plane * local):
                share[k, t, part] = raws[c][code[0, my_z * plane * local + t]]

        @pl.when(outer)
        def _():
            p_copy(c).wait_recv()

        for d in range(1, plane):
            m_copy(c, d).start()
        held[k, :, part, my_rows] = share[k, pl.ds(my_q * local, local), part]

    def arrived(c):
        for d in range(1, plane):
            m_arrival(c, d).wait_recv()

    def place(k, keys, values):
        for j in range(local):
            keys[j, new_len:] = held[k, j, 0]
            values[j, new_len:] = held[k, j, 1]

    def begin(k):
        for copy in loads(k, k, hbm, buf, isem):
            copy.wait()
        place(k, kbuf.at[k], vbuf.at[k])

    def attend_some(k, lo, hi):
        def one(j, inside):
            attend(k, j, buf)
            return inside

        lax.fori_loop(lo, hi, one, 0, unroll=True)

    pass_on(0)

    def step(k, carry):
        for later in range(1, front):
            pl.when(k + 1 == later)(functools.partial(pass_on, later))
        for c in range(front - 1):
            pl.when(k == c)(functools.partial(arrived, c))
        begin(k)
        attend_some(k, 0, local)
        return carry

    lax.fori_loop(0, front - 1, step, 0)
    pass_on(front)
    arrived(front - 1)
    begin(front - 1)
    attend_some(front - 1, 0, local // 2)
    pass_on(front + 1)
    attend_some(front - 1, local // 2, local)
    for copy in last_loads():
        copy.wait()
    arrived(front)
    arrived(front + 1)
    place(heads - 1, klast.at[0], vlast.at[0])

    for c in range(len(chunks)):
        for d in range(1, plane):
            a_copy(c, d).wait_send()
            m_copy(c, d).wait_send()

        @pl.when(outer)
        def _():
            z_copy(c, 0, nz - 1 - near).wait_send()
            z_copy(c, 1, near).wait_send()

        @pl.when(inner)
        def _():
            z_copy(c, 0, nz - 1 - my_z).wait_send()
            p_copy(c).wait_send()

    def r_finish(d, carry):
        r_arrival(d).wait_recv()
        r_copy(d).wait_send()
        return carry

    lax.fori_loop(1, n, r_finish, 0)


def close_kernel(
    parents, rewards, part, qlast, klast, vlast, out_hbm, shares, obuf, psem, osem
):
    front, local, _, width = part.shape
    children = parents.shape[1]

    def move(k):
        return pltpu.make_async_copy(
            part.at[k], out_hbm.at[:, :, pl.ds(k * width, width)], psem.at[k]
        )

    def put(j):
        return pltpu.make_async_copy(
            obuf.at[0, j], out_hbm.at[j, :, pl.ds(front * width, width)], osem.at[j]
        )

    for k in range(front):
        move(k).start()
    me = lax.axis_index("beam")
    ids = parents[...]
    reward = rewards[:, :, :children]
    beam = lax.broadcasted_iota(jnp.int32, reward.shape, 0) * local
    beam = beam + lax.broadcasted_iota(jnp.int32, reward.shape, 1)
    given = jnp.where(beam == ids[None], reward, 0.0)
    given = jnp.sum(jnp.sum(given, axis=0), axis=0, keepdims=True)
    part_of = children * given / jnp.sum(given, axis=1, keepdims=True)
    lane = lax.broadcasted_iota(jnp.int32, part_of.shape, 1)
    for j in range(local):
        shares[j] = jnp.sum(jnp.where(lane == me * local + j, part_of, 0.0))
    for j in range(local):
        attend(0, j, (qlast, klast, vlast, obuf))
        put(j).start()
    for k in range(front):
        move(k).wait()
    for j in range(local):
        put(j).wait()


def plane_body(queries, new_keys, new_values, step_kv, prm_last, value_head, parents):
    n = lax.axis_size("beam")
    ny, nz = 2, 4
    plane = 2 * ny
    local, new_len, qwidth = queries.shape
    step_len, kv_width = step_kv.shape[2:]
    heads = kv_width // HEAD_SIZE
    width = qwidth // heads
    rows = step_len // plane
    front = heads - 1
    chunks = halves(heads)
    many = len(chunks)
    total = new_len + step_len
    dma = pltpu.SemaphoreType.DMA
    bf16 = jnp.bfloat16
    vmem = pl.BlockSpec(memory_space=pltpu.VMEM)
    smem = pl.BlockSpec(memory_space=pltpu.SMEM)
    anywhere = pl.BlockSpec(memory_space=pl.ANY)
    row = parents.reshape(1, -1)
    part, rewards, qlast, klast, vlast = pl.pallas_call(
        functools.partial(plane_kernel, nz),
        out_shape=(
            pltpu.VMEM((front, local, new_len, width), bf16),
            pltpu.VMEM((n, local, 128), jnp.float32),
            pltpu.VMEM((1, local, new_len, width), bf16),
            pltpu.VMEM((1, local, total, HEAD_SIZE), bf16),
            pltpu.VMEM((1, local, total, HEAD_SIZE), bf16),
        ),
        in_specs=[smem] + [vmem] * 4 + [anywhere] * 3,
        out_specs=(vmem,) * 5,
        scratch_shapes=[
            pltpu.VMEM((n * KEEP, count, rows, HEAD_SIZE), bf16)
            for _, _, count in chunks
        ]
        + [
            pltpu.VMEM((heads, plane, KEEP, 2, rows, HEAD_SIZE), bf16),
            pltpu.VMEM((heads, plane * local, 2, rows, HEAD_SIZE), bf16),
            pltpu.VMEM((heads, plane * local, 2, rows, HEAD_SIZE), bf16),
            pltpu.VMEM((heads, local, 2, step_len, HEAD_SIZE), bf16),
            pltpu.VMEM((front, local, new_len, width), bf16),
            pltpu.VMEM((front, local, total, HEAD_SIZE), bf16),
            pltpu.VMEM((front, local, total, HEAD_SIZE), bf16),
            pltpu.VMEM(row.shape, jnp.int32),
            pltpu.SMEM(row.shape, jnp.int32),
            dma((n,)), dma((n,)),
            dma((many, plane)), dma((many, plane)),
            dma((many, 2)), dma((many, nz)),
            dma((many,)), dma((many,)),
            dma((many, plane)), dma((many, plane)),
            dma((heads, 5)), dma,
        ],
        compiler_params=pltpu.CompilerParams(
            collective_id=0, has_side_effects=True, vmem_limit_bytes=44 << 20
        ),
    )(
        parents, row, prm_last, value_head.reshape(1, -1), step_kv, queries,
        new_keys, new_values,
    )
    return pl.pallas_call(
        close_kernel,
        out_shape=(
            jax.ShapeDtypeStruct(queries.shape, bf16),
            jax.ShapeDtypeStruct((local,), jnp.float32),
        ),
        in_specs=[vmem] * 6,
        out_specs=(anywhere, smem),
        scratch_shapes=[
            pltpu.VMEM((1, local, new_len, width), bf16),
            dma((front,)), dma((local,)),
        ],
        compiler_params=pltpu.CompilerParams(vmem_limit_bytes=24 << 20),
    )(row, rewards, part, qlast, klast, vlast)


def line_body(queries, new_keys, new_values, step_kv, prm_last, value_head, parents):
    n = lax.axis_size("beam")
    ny = 1
    nz = n // (2 * ny)
    me = lax.axis_index("beam")
    local, new_len, qwidth = queries.shape
    children = parents.shape[0]
    step_len, kv_width = step_kv.shape[2:]
    heads = kv_width // HEAD_SIZE
    width = qwidth // heads

    beams = jnp.arange(n * local, dtype=jnp.int32)
    equal = parents[None, :] == beams[:, None]
    hits = jnp.sum(equal.astype(jnp.int32), axis=1)
    kept = (hits > 0).astype(jnp.int32)
    before = jnp.sum(kept[None, :] * (beams[None, :] < beams[:, None]), axis=1)
    rank_of_beam = before % KEEP
    wanted = (
        (beams[None, :] // local == me)
        & (kept[None, :] > 0)
        & (rank_of_beam[None, :] == jnp.arange(KEEP, dtype=jnp.int32)[:, None])
    )
    keep_pos = jnp.sum(wanted * (beams % local)[None, :], axis=1).astype(jnp.int32)
    rank = jnp.sum(equal * rank_of_beam[:, None], axis=0)
    owner = parents // local
    c, y, z = owner % 2, (owner // 2) % ny, owner // (2 * ny)
    my_c, my_y = me % 2, (me // 2) % ny
    code = jnp.where(y == my_y, ((c != my_c) * nz + z) * KEEP + rank, -1).astype(jnp.int32)
    y_peer = me + 2 - 4 * my_y if ny > 1 else me
    own = lax.dynamic_slice_in_dim(code, me * local, local)
    other = lax.dynamic_slice_in_dim(code, y_peer * local, local)
    idx = jnp.concatenate([keep_pos, own, other])

    dma = pltpu.SemaphoreType.DMA
    bf16 = jnp.bfloat16
    vmem = pl.BlockSpec(memory_space=pltpu.VMEM)
    anywhere = pl.BlockSpec(memory_space=pl.ANY)
    last = 2
    front = heads - last
    part, rewards, tail = pl.pallas_call(
        functools.partial(kernel, n, ny, nz),
        out_shape=(
            jax.ShapeDtypeStruct((local, new_len, front * width), bf16),
            jax.ShapeDtypeStruct((n, local, 128), jnp.float32),
            jax.ShapeDtypeStruct((last, local, 2, step_len, HEAD_SIZE), bf16),
        ),
        in_specs=[pl.BlockSpec(memory_space=pltpu.SMEM), vmem, vmem, vmem]
        + [anywhere] * 3,
        out_specs=(anywhere, vmem, vmem),
        scratch_shapes=[
            pltpu.VMEM((heads, 2, nz, KEEP, 2, step_len, HEAD_SIZE), bf16),
            pltpu.VMEM((heads, local, 2, step_len, HEAD_SIZE), bf16),
            pltpu.VMEM((heads, local, 2, step_len, HEAD_SIZE), bf16),
            pltpu.VMEM((front, local, new_len, width), bf16),
            pltpu.VMEM((front, local, new_len + step_len, HEAD_SIZE), bf16),
            pltpu.VMEM((front, local, new_len + step_len, HEAD_SIZE), bf16),
            pltpu.VMEM((front, local, new_len, width), bf16),
            dma((n,)), dma((n,)),
            dma((heads, nz)), dma((heads, nz)), dma((heads,)),
            dma((heads,)), dma((heads,)),
            dma((heads,)), dma((heads,)),
            dma((front, 5)), dma((front,)),
        ],
        compiler_params=pltpu.CompilerParams(
            collective_id=0, has_side_effects=True, vmem_limit_bytes=56 << 20
        ),
    )(idx, prm_last, value_head.reshape(1, -1), step_kv, queries, new_keys, new_values)

    attended = pl.pallas_call(
        functools.partial(last_kernel, front),
        out_shape=jax.ShapeDtypeStruct(queries.shape, bf16),
        in_specs=[vmem] + [anywhere] * 4,
        out_specs=anywhere,
        scratch_shapes=[
            pltpu.VMEM((last, local, new_len, width), bf16),
            pltpu.VMEM((last, local, new_len + step_len, HEAD_SIZE), bf16),
            pltpu.VMEM((last, local, new_len + step_len, HEAD_SIZE), bf16),
            pltpu.VMEM((last, local, new_len, width), bf16),
            pltpu.VMEM((local, new_len, front * width), bf16),
            dma((last, 5)), dma((last,)), dma((local,)), dma((local,)),
        ],
        compiler_params=pltpu.CompilerParams(vmem_limit_bytes=56 << 20),
    )(tail, part, queries, new_keys, new_values)

    reward = rewards[:, :, 0].reshape(-1)
    total = jnp.sum(reward * hits.astype(jnp.float32))
    mine = lax.dynamic_slice_in_dim(parents, me * local, local)
    match = mine[:, None] == beams[None, :]
    child_reward = jnp.sum(jnp.where(match, reward[None, :], 0.0), axis=1)
    child_share = children * child_reward / total
    return (attended, child_share)


def solution(mesh):
    in_specs = (
        P(("prompts", "beam"), None, None),
        P(("prompts", "beam"), None, None),
        P(("prompts", "beam"), None, None),
        P(("prompts", "beam"), None, None, None),
        P(("prompts", "beam"), None),
        P(),
        P("prompts"),
    )
    out_specs = (P(("prompts", "beam"), None, None), P(("prompts", "beam")))
    body = plane_body if mesh.shape["beam"] == 16 else line_body
    return jax.shard_map(body, mesh=mesh, in_specs=in_specs, out_specs=out_specs, check_vma=False)
```

```python
import functools

import jax
import jax.numpy as jnp
from jax import lax
from jax.experimental import pallas as pl
from jax.experimental.pallas import tpu as pltpu
from jax.sharding import PartitionSpec as P

HEAD_SIZE = 128
KEEP = 2
LOG2E = 1.4426950408889634


def remote(src, dst, send, recv, device):
    return pltpu.make_async_remote_copy(
        src_ref=src, dst_ref=dst, send_sem=send, recv_sem=recv,
        device_id={"beam": device}, device_id_type=pl.DeviceIdType.MESH,
    )


def loads(k, head, hbm, buf, isem):
    q_hbm, nk_hbm, nv_hbm = hbm
    qbuf, kbuf, vbuf, _ = buf
    width = qbuf.shape[3]
    half = q_hbm.shape[1] // 2
    cols = pl.ds(pl.multiple_of(head * HEAD_SIZE, HEAD_SIZE), HEAD_SIZE)
    wide = pl.ds(pl.multiple_of(head * width, width), width)
    lo, hi = pl.ds(0, half), pl.ds(half, half)
    return [
        pltpu.make_async_copy(q_hbm.at[:, :, wide], qbuf.at[k], isem.at[k, 0]),
        pltpu.make_async_copy(nk_hbm.at[:, hi, cols], kbuf.at[k, :, lo], isem.at[k, 1]),
        pltpu.make_async_copy(nk_hbm.at[:, lo, cols], kbuf.at[k, :, hi], isem.at[k, 2]),
        pltpu.make_async_copy(nv_hbm.at[:, hi, cols], vbuf.at[k, :, lo], isem.at[k, 3]),
        pltpu.make_async_copy(nv_hbm.at[:, lo, cols], vbuf.at[k, :, hi], isem.at[k, 4]),
    ]


def store(k, head, obuf, out_hbm, osem):
    width = obuf.shape[3]
    wide = pl.ds(pl.multiple_of(head * width, width), width)
    return pltpu.make_async_copy(obuf.at[k], out_hbm.at[:, :, wide], osem.at[k])


def attend(k, j, buf):
    qbuf, kbuf, vbuf, obuf = buf
    half = qbuf.shape[2] // 2
    group = qbuf.shape[3] // HEAD_SIZE
    row = lax.rem(lax.broadcasted_iota(jnp.int32, (group * half, half), 0), half)
    column = lax.broadcasted_iota(jnp.int32, (group * half, half), 1)
    visible = column <= row
    scale = HEAD_SIZE ** (-0.5) * LOG2E
    for part in range(2):
        start = half if part == 0 else 0
        keys = kbuf[k, j, start:]
        values = vbuf[k, j, start:]
        values = jnp.concatenate([values, jnp.ones_like(values)], axis=1)
        rows = slice(part * half, (part + 1) * half)
        query = jnp.concatenate(
            [qbuf[k, j, rows, g * HEAD_SIZE:(g + 1) * HEAD_SIZE] for g in range(group)],
            axis=0,
        )
        s = lax.dot_general(
            query, keys, (((1,), (1,)), ((), ())), preferred_element_type=jnp.float32
        )
        s = jnp.concatenate(
            [jnp.where(visible, s[:, :half], -jnp.inf), s[:, half:]], axis=1
        )
        top = jnp.max(s, axis=1, keepdims=True)
        p = jnp.exp2((s - top) * scale).astype(jnp.bfloat16)
        o = jnp.dot(p, values, preferred_element_type=jnp.float32)
        o = (o[:, :HEAD_SIZE] / o[:, HEAD_SIZE:]).astype(jnp.bfloat16)
        for g in range(group):
            obuf[k, j, rows, g * HEAD_SIZE:(g + 1) * HEAD_SIZE] = o[
                g * half:(g + 1) * half
            ]


def last_kernel(
    first, tail, part, q_hbm, nk_hbm, nv_hbm, out_hbm,
    qbuf, kbuf, vbuf, obuf, held, isem, osem, hin, hout,
):
    hbm = (q_hbm, nk_hbm, nv_hbm)
    buf = (qbuf, kbuf, vbuf, obuf)
    local, new_len, done = held.shape
    count = qbuf.shape[0]

    def fetch(j):
        return pltpu.make_async_copy(part.at[j], held.at[j], hin.at[j])

    def put(j):
        return pltpu.make_async_copy(
            held.at[j], out_hbm.at[j, :, pl.ds(0, done)], hout.at[j]
        )

    for k in range(count):
        for copy in loads(k, first + k, hbm, buf, isem):
            copy.start()
        if k == 0:
            for j in range(local):
                fetch(j).start()
    for k in range(count):
        for j in range(local):
            kbuf[k, j, new_len:] = tail[k, j, 0]
            vbuf[k, j, new_len:] = tail[k, j, 1]
    for k in range(count):
        for copy in loads(k, first + k, hbm, buf, isem):
            copy.wait()
        if k > 0:
            for j in range(local):
                fetch(j).wait()
                put(j).start()

        def one(j, carry):
            attend(k, j, buf)
            return carry

        lax.fori_loop(0, local, one, 0, unroll=2)
        store(k, first + k, obuf, out_hbm, osem).start()
    for j in range(local):
        put(j).wait()
    for k in range(count):
        store(k, first + k, obuf, out_hbm, osem).wait()


def kernel(
    n, ny, nz, idx, prm, head, kv, q_hbm, nk_hbm, nv_hbm, out_hbm, rbuf, tail,
    col, pbuf, ybuf, qbuf, kbuf, vbuf, obuf,
    rsend, rrecv, zsend, zrecv, lsend, csend, crecv, ysend, yrecv, isem, osem,
):
    me = lax.axis_index("beam")
    my_c = lax.rem(me, 2)
    my_y = lax.rem(lax.div(me, 2), ny)
    my_z = lax.div(me, 2 * ny)
    local = kv.shape[0]
    step_len = kv.shape[2]
    heads = kv.shape[3] // HEAD_SIZE
    new_len = q_hbm.shape[1]
    front = qbuf.shape[0]
    hbm = (q_hbm, nk_hbm, nv_hbm)
    buf = (qbuf, kbuf, vbuf, obuf)

    def at(z, y, c):
        return (z * ny + y) * 2 + c

    core_peer = at(my_z, my_y, 1 - my_c)
    y_peer = at(my_z, lax.rem(my_y + 1, ny), my_c)

    barrier = pltpu.get_barrier_semaphore()

    def greet(d, carry):
        pl.semaphore_signal(
            barrier, inc=1, device_id={"beam": lax.rem(me + d, n)},
            device_id_type=pl.DeviceIdType.MESH,
        )
        return carry

    lax.fori_loop(1, n, greet, 0)

    def load(k, carry):
        for copy in loads(k, k, hbm, buf, isem):
            copy.start()
        return carry

    lax.fori_loop(0, front, load, 0)

    for k in range(heads):
        cols = slice(k * HEAD_SIZE, (k + 1) * HEAD_SIZE)
        for r in range(KEEP):
            tile = kv[0, :, :, cols]
            for b in range(1, local):
                tile = jnp.where(idx[r] == b, kv[b, :, :, cols], tile)
            col[k, 0, my_z, r] = tile

    hidden = prm[...].astype(jnp.float32)
    square = jnp.mean(hidden * hidden, axis=-1, keepdims=True)
    normed = hidden * lax.rsqrt(square + 1e-05)
    score = jnp.sum(normed * head[...], axis=-1, keepdims=True)
    reward = (1.0 / (1.0 + jnp.exp(-score))).astype(jnp.bfloat16).astype(jnp.float32)
    rbuf[me] = jnp.broadcast_to(reward, (local, 128))

    pl.semaphore_wait(barrier, n - 1)

    def z_copy(k, d):
        zt = lax.rem(my_z + d, nz)
        return remote(
            col.at[k, 0, my_z], col.at[k, 0, my_z],
            zsend.at[k, d], zrecv.at[k, my_z], at(zt, my_y, my_c),
        )

    def z_arrival(k, d):
        zs = lax.rem(my_z + d, nz)
        return remote(
            col.at[k, 0, zs], col.at[k, 0, zs],
            zsend.at[k, d], zrecv.at[k, zs], at(zs, my_y, my_c),
        )

    relayed = nz == 4

    def when_direct(d, run):
        if relayed and d == 1:
            pl.when(my_z != nz - 1)(run)
        elif relayed and d == nz - 1:
            pl.when(my_z != 0)(run)
        else:
            run()

    def relay_copy(k, source, target):
        return remote(
            col.at[k, 0, source], col.at[k, 0, source],
            lsend.at[k], zrecv.at[k, source], at(target, my_y, my_c),
        )

    ends = ((nz - 2, 0, nz - 1), (1, nz - 1, 0)) if relayed else ()

    def relay(k):
        for who, source, target in ends:

            @pl.when(my_z == who)
            def _():
                relay_copy(k, source, target).wait_recv()
                relay_copy(k, source, target).start()

    def z_wait(k):
        for d in range(1, nz):
            zs = lax.rem(my_z + d, nz)
            got = (my_z == 1) & (zs == nz - 1) | (my_z == nz - 2) & (zs == 0)
            if relayed:

                @pl.when(jnp.logical_not(got))
                def _():
                    z_arrival(k, d).wait_recv()
            else:
                z_arrival(k, d).wait_recv()

    def z_start(k, carry):
        for d in range(1, nz):
            when_direct(d, z_copy(k, d).start)
        return carry

    def r_copy(d):
        return remote(rbuf.at[me], rbuf.at[me], rsend.at[d], rrecv.at[me], lax.rem(me + d, n))

    def r_arrival(d):
        src = lax.rem(me + d, n)
        return remote(rbuf.at[src], rbuf.at[src], rsend.at[d], rrecv.at[src], src)

    lax.fori_loop(0, heads, z_start, 0)

    def r_start(d, carry):
        r_copy(d).start()
        return carry

    lax.fori_loop(1, n, r_start, 0)

    def c_copy(k):
        return remote(col.at[k, 0], col.at[k, 1], csend.at[k], crecv.at[k], core_peer)

    def y_copy(k):
        return remote(pbuf.at[k], ybuf.at[k], ysend.at[k], yrecv.at[k], y_peer)

    def pick(k, codes, bases):
        tiles = list(bases)
        for c in range(2):
            for z in range(nz):
                for r in range(KEEP):
                    entry = col[k, c, z, r]
                    slot = (c * nz + z) * KEEP + r
                    tiles = [
                        jnp.where(code == slot, entry, tile)
                        for code, tile in zip(codes, tiles)
                    ]
        return tiles

    def exchange_one(k):
        z_wait(k)
        c_copy(k).start()

    def exchange_two(k):
        c_copy(k).wait_recv()
        if ny > 1:
            codes = [idx[KEEP + local + j] for j in range(local)]
            tiles = pick(k, codes, [col[k, 0, 0, 0]] * local)
            for j in range(local):
                pbuf[k, j] = tiles[j]
            y_copy(k).start()

    def parents_of(k):
        if ny > 1:
            y_copy(k).wait_recv()
        bases = [ybuf[k, j] if ny > 1 else col[k, 0, 0, 0] for j in range(local)]
        return pick(k, [idx[KEEP + j] for j in range(local)], bases)

    def place(k):
        tiles = parents_of(k)
        for j in range(local):
            kbuf[k, j, new_len:] = tiles[j][0]
            vbuf[k, j, new_len:] = tiles[j][1]

    def attend_some(k, first, last):
        def one(j, carry):
            attend(k, j, buf)
            return carry

        lax.fori_loop(first, last, one, 0, unroll=True)

    def ready(k):
        for copy in loads(k, k, hbm, buf, isem):
            copy.wait()
        place(k)

    def finish_head(k):
        attend_some(k, local // 2, local)
        store(k, k, obuf, out_hbm, osem).start()

    def start_head(k):
        ready(k)
        attend_some(k, 0, local // 2)

    relay(0)
    exchange_one(0)
    relay(1)
    exchange_one(1)
    exchange_two(0)
    relay(2)

    def step(k, carry):
        exchange_one(k)
        exchange_two(k - 1)
        pl.when(k + 1 < heads)(functools.partial(relay, k + 1))
        start_head(k - 2)
        finish_head(k - 2)
        return carry

    lax.fori_loop(2, heads, step, 0)
    exchange_two(heads - 1)
    for k in range(front, heads):
        tiles = parents_of(k)
        for j in range(local):
            tail[k - front, j] = tiles[j]

    def finish(k, carry):
        for d in range(1, nz):
            when_direct(d, z_copy(k, d).wait_send)
        for who, source, target in ends:
            pl.when(my_z == who)(relay_copy(k, source, target).wait_send)
        c_copy(k).wait_send()
        if ny > 1:
            y_copy(k).wait_send()
        return carry

    lax.fori_loop(0, heads, finish, 0)

    def stored(k, carry):
        store(k, k, obuf, out_hbm, osem).wait()
        return carry

    lax.fori_loop(0, front, stored, 0)

    def r_finish(d, carry):
        r_arrival(d).wait_recv()
        r_copy(d).wait_send()
        return carry

    lax.fori_loop(1, n, r_finish, 0)


def halves(heads):
    return [(k, 0, 2) for k in range(heads - 1)] + [(heads - 1, 0, 1), (heads - 1, 1, 1)]


def plane_kernel(
    nz, row_hbm, prm_hbm, head_hbm, kv_hbm, q_hbm, nk_hbm, nv_hbm,
    obuf, shares, qlast, klast, vlast, *scratch
):
    local, _, step_len, kv_width = kv_hbm.shape
    heads = kv_width // HEAD_SIZE
    chunks = halves(heads)
    raws = scratch[:len(chunks)]
    (
        kept, picked, share, held, qbuf, kbuf, vbuf, rbuf,
        row, prm, head, kv, crow, listed, code,
        rsend, rrecv, asend, arecv, zsend, zrecv, fsend, frecv, psend,
        msend, mrecv, isem, csem,
    ) = scratch[len(chunks):]
    me = lax.axis_index("beam")
    plane = kept.shape[1]
    n = nz * plane
    rows = step_len // plane
    new_len = q_hbm.shape[1]
    front = qbuf.shape[0]
    hbm = (q_hbm, nk_hbm, nv_hbm)
    buf = (qbuf, kbuf, vbuf, obuf)
    my_q = lax.rem(me, plane)
    my_z = lax.div(me, plane)
    inner = (my_z == 1) | (my_z == 2)
    outer = jnp.logical_not(inner)
    near = jnp.where(my_z < 2, 1 - my_z, 5 - my_z)
    my_rows = pl.ds(pl.multiple_of(my_q * rows, rows), rows)

    inputs = [
        pltpu.make_async_copy(src, dst, csem.at[i])
        for i, (src, dst) in enumerate(
            [(row_hbm, listed), (kv_hbm, kv), (row_hbm, row), (prm_hbm, prm), (head_hbm, head)]
        )
    ]
    for copy in inputs:
        copy.start()

    barrier = pltpu.get_barrier_semaphore()

    def greet(d, carry):
        pl.semaphore_signal(
            barrier, inc=1, device_id={"beam": lax.rem(me + d, n)},
            device_id_type=pl.DeviceIdType.MESH,
        )
        return carry

    lax.fori_loop(1, n, greet, 0)

    inputs[0].wait()
    low, high = local - 1, 0
    for c in range(listed.shape[1]):
        spot = listed[0, c] - me * local
        mine = (spot >= 0) & (spot < local)
        low = jnp.where(mine, jnp.minimum(low, spot), low)
        high = jnp.where(mine, jnp.maximum(high, spot), high)
    inputs[1].wait()

    def keep(c):
        k, lo, count = chunks[c]
        cols = slice(k * HEAD_SIZE, (k + 1) * HEAD_SIZE)
        part = slice(lo, lo + count)
        for r, beam in enumerate((low, high)):
            raws[c][me * KEEP + r] = kv[beam, part, my_rows, cols]
            for q in range(plane):
                kept[k, q, r, part] = kv[beam, part, q * rows:(q + 1) * rows, cols]

    keep(0)
    pl.semaphore_wait(barrier, n - 1)

    def mate(d):
        if d == 1:
            return my_q + 1 - 2 * lax.rem(my_q, 2)
        return lax.rem(my_q + 2, plane) if d == 2 else plane - 1 - my_q

    def a_part(c, q, source):
        k, lo, count = chunks[c]
        slot = pl.ds((my_z * plane + source) * KEEP, KEEP)
        return kept.at[k, q, :, pl.ds(lo, count)], raws[c].at[slot]

    def a_copy(c, d):
        src, dst = a_part(c, mate(d), my_q)
        return remote(
            src, dst, asend.at[c, d], arecv.at[c, my_q], my_z * plane + mate(d)
        )

    def a_arrival(c, d):
        src, dst = a_part(c, mate(d), mate(d))
        return remote(
            src, dst, asend.at[c, d], arecv.at[c, mate(d)], my_z * plane + mate(d)
        )

    def z_copy(c, i, target):
        slot = pl.ds(my_z * plane * KEEP, plane * KEEP)
        return remote(
            raws[c].at[slot], raws[c].at[slot], zsend.at[c, i], zrecv.at[c, my_z],
            target * plane + my_q,
        )

    def z_arrival(c, d):
        z = lax.rem(my_z + d, nz)
        slot = pl.ds(z * plane * KEEP, plane * KEEP)
        return remote(
            raws[c].at[slot], raws[c].at[slot], zsend.at[c, 0], zrecv.at[c, z],
            z * plane + my_q,
        )

    def f_copy(q, i, target):
        slot = pl.ds((my_z * plane + q) * KEEP, KEEP)
        return remote(
            raws[0].at[slot], raws[0].at[slot], fsend.at[i, q], frecv.at[my_z, q],
            target * plane + my_q,
        )

    def f_arrival(d, q):
        z = lax.rem(my_z + d, nz)
        slot = pl.ds((z * plane + q) * KEEP, KEEP)
        return remote(
            raws[0].at[slot], raws[0].at[slot], fsend.at[0, q], frecv.at[z, q],
            z * plane + my_q,
        )

    def along(do):
        @pl.when(outer)
        def _():
            do(0, nz - 1 - near)
            do(1, near)

        @pl.when(inner)
        def _():
            do(0, nz - 1 - my_z)

    def slices(c, source):
        k, lo, count = chunks[c]
        part = pl.ds(lo, count)
        theirs = pl.ds(pl.multiple_of(source * rows, rows), rows)
        return k, part, held.at[k, :, part, theirs]

    def p_copy(c, q):
        k, part, dst = slices(c, my_q)
        return remote(
            picked.at[k, pl.ds(q * local, local), part], dst,
            psend.at[c, q], mrecv.at[c, my_q], near * plane + q,
        )

    def p_arrival(c, q):
        k, part, dst = slices(c, q)
        return remote(
            picked.at[k, pl.ds(q * local, local), part], dst,
            psend.at[c, q], mrecv.at[c, q], near * plane + q,
        )

    def m_copy(c, d):
        k, part, dst = slices(c, my_q)
        q = mate(d)
        return remote(
            share.at[k, pl.ds(q * local, local), part], dst,
            msend.at[c, d], mrecv.at[c, my_q], my_z * plane + q,
        )

    def m_arrival(c, d):
        q = mate(d)
        k, part, dst = slices(c, q)
        return remote(
            share.at[k, pl.ds(q * local, local), part], dst,
            msend.at[c, d], mrecv.at[c, q], my_z * plane + q,
        )

    def r_copy(d):
        return remote(rbuf.at[me], rbuf.at[me], rsend.at[d], rrecv.at[me], lax.rem(me + d, n))

    def r_arrival(d):
        src = lax.rem(me + d, n)
        return remote(rbuf.at[src], rbuf.at[src], rsend.at[d], rrecv.at[src], src)

    def a_start(c):
        for d in range(1, plane):
            a_copy(c, d).start()

    along(lambda i, target: f_copy(my_q, i, target).start())
    a_start(0)
    for c in range(1, len(chunks)):
        keep(c)
        a_start(c)
    for d in range(1, plane):
        a_arrival(0, d).wait_recv()
        along(lambda i, target: f_copy(mate(d), i, target).start())
    for c in range(1, len(chunks)):
        for d in range(1, plane):
            a_arrival(c, d).wait_recv()
        along(lambda i, target: z_copy(c, i, target).start())

    inputs[2].wait()
    ids = row[...]
    owner = lax.div(ids, local)
    groups = lax.broadcasted_iota(jnp.int32, (n, ids.shape[1]), 0)
    own = groups == owner
    first = jnp.min(jnp.where(own, ids, n * local), axis=1, keepdims=True)
    first = jnp.min(jnp.where(own, first, n * local), axis=0, keepdims=True)
    crow[...] = owner * KEEP + (ids > first).astype(jnp.int32)
    numbers = pltpu.make_async_copy(crow, code, csem.at[len(inputs)])
    numbers.start()

    def last_loads():
        return loads(0, heads - 1, hbm, (qlast, klast, vlast, None), isem.at[pl.ds(front, 1)])

    def load(k, carry):
        for copy in loads(k, k, hbm, buf, isem):
            copy.start()
        return carry

    lax.fori_loop(0, front, load, 0)
    for copy in last_loads():
        copy.start()

    inputs[3].wait()
    inputs[4].wait()
    hidden = prm[...].astype(jnp.float32)
    square = jnp.mean(hidden * hidden, axis=-1, keepdims=True)
    normed = hidden * lax.rsqrt(square + 1e-05)
    score = jnp.sum(normed * head[...], axis=-1, keepdims=True)
    reward = (1.0 / (1.0 + jnp.exp(-score))).astype(jnp.bfloat16).astype(jnp.float32)
    rbuf[me] = jnp.broadcast_to(reward, (local, 128))

    def r_start(d, carry):
        r_copy(d).start()
        return carry

    lax.fori_loop(1, n, r_start, 0)
    numbers.wait()

    def pass_on(c):
        k, lo, count = chunks[c]
        part = slice(lo, lo + count)

        @pl.when(inner)
        def _():
            for d in range(1, nz):
                if c == 0:
                    for q in range(plane):
                        f_arrival(d, q).wait_recv()
                else:
                    z_arrival(c, d).wait_recv()
            for q in range(plane):
                for t in range(q * local, (q + 1) * local):
                    picked[k, t, part] = raws[c][code[0, near * plane * local + t]]
                p_copy(c, q).start()
            for t in range(plane * local):
                share[k, t, part] = raws[c][code[0, my_z * plane * local + t]]
            for d in range(1, plane):
                m_copy(c, d).start()
            held[k, :, part, my_rows] = share[k, pl.ds(my_q * local, local), part]

    def arrived(c):
        @pl.when(inner)
        def _():
            for d in range(1, plane):
                m_arrival(c, d).wait_recv()

        @pl.when(outer)
        def _():
            for q in range(plane):
                p_arrival(c, q).wait_recv()

    def place(k, keys, values):
        for j in range(local):
            keys[j, new_len:] = held[k, j, 0]
            values[j, new_len:] = held[k, j, 1]

    def begin(k):
        for copy in loads(k, k, hbm, buf, isem):
            copy.wait()
        place(k, kbuf.at[k], vbuf.at[k])

    def attend_some(k, lo, hi):
        def one(j, inside):
            attend(k, j, buf)
            return inside

        lax.fori_loop(lo, hi, one, 0, unroll=True)

    pass_on(0)

    def step(k, carry):
        for later in range(1, front):
            pl.when(k + 1 == later)(functools.partial(pass_on, later))
        for c in range(front - 1):
            pl.when(k == c)(functools.partial(arrived, c))
        begin(k)
        attend_some(k, 0, local)
        return carry

    lax.fori_loop(0, front - 1, step, 0)

    def r_finish(d, carry):
        r_arrival(d).wait_recv()
        r_copy(d).wait_send()
        return carry

    lax.fori_loop(1, n, r_finish, 0)
    reward = rbuf[:, :, :ids.shape[1]]
    beam = lax.broadcasted_iota(jnp.int32, reward.shape, 0) * local
    beam = beam + lax.broadcasted_iota(jnp.int32, reward.shape, 1)
    given = jnp.where(beam == row[...][None], reward, 0.0)
    given = jnp.sum(jnp.sum(given, axis=0), axis=0, keepdims=True)
    shares[...] = ids.shape[1] * given / jnp.sum(given, axis=1, keepdims=True)

    pass_on(front)
    arrived(front - 1)
    begin(front - 1)
    attend_some(front - 1, 0, local // 2)
    pass_on(front + 1)
    attend_some(front - 1, local // 2, local)
    for copy in last_loads():
        copy.wait()
    arrived(front)
    arrived(front + 1)
    place(heads - 1, klast.at[0], vlast.at[0])

    along(lambda i, target: [f_copy(q, i, target).wait_send() for q in range(plane)])
    for c in range(len(chunks)):
        for d in range(1, plane):
            a_copy(c, d).wait_send()
        if c > 0:
            along(lambda i, target: z_copy(c, i, target).wait_send())

        @pl.when(inner)
        def _():
            for q in range(plane):
                p_copy(c, q).wait_send()
            for d in range(1, plane):
                m_copy(c, d).wait_send()


def close_kernel(
    shares, part, qlast, klast, vlast, out_hbm, mine, obuf, psem, osem
):
    front, local, _, width = part.shape

    def move(k):
        return pltpu.make_async_copy(
            part.at[k], out_hbm.at[:, :, pl.ds(k * width, width)], psem.at[k]
        )

    def put(j):
        return pltpu.make_async_copy(
            obuf.at[0, j], out_hbm.at[j, :, pl.ds(front * width, width)], osem.at[j]
        )

    for k in range(front):
        move(k).start()
    me = lax.axis_index("beam")
    all_shares = shares[...]
    lane = lax.broadcasted_iota(jnp.int32, all_shares.shape, 1)
    for j in range(local):
        mine[j] = jnp.sum(jnp.where(lane == me * local + j, all_shares, 0.0))
    for j in range(local):
        attend(0, j, (qlast, klast, vlast, obuf))
        put(j).start()
    for k in range(front):
        move(k).wait()
    for j in range(local):
        put(j).wait()


def plane_body(queries, new_keys, new_values, step_kv, prm_last, value_head, parents):
    n = lax.axis_size("beam")
    ny, nz = 2, 4
    plane = 2 * ny
    local, new_len, qwidth = queries.shape
    step_len, kv_width = step_kv.shape[2:]
    heads = kv_width // HEAD_SIZE
    width = qwidth // heads
    rows = step_len // plane
    front = heads - 1
    chunks = halves(heads)
    many = len(chunks)
    total = new_len + step_len
    dma = pltpu.SemaphoreType.DMA
    bf16 = jnp.bfloat16
    vmem = pl.BlockSpec(memory_space=pltpu.VMEM)
    smem = pl.BlockSpec(memory_space=pltpu.SMEM)
    in_hbm = pl.BlockSpec(memory_space=pltpu.HBM)
    anywhere = pl.BlockSpec(memory_space=pl.ANY)
    row = parents.reshape(1, -1)
    part, shares, qlast, klast, vlast = pl.pallas_call(
        functools.partial(plane_kernel, nz),
        out_shape=(
            pltpu.VMEM((front, local, new_len, width), bf16),
            pltpu.VMEM(row.shape, jnp.float32),
            pltpu.VMEM((1, local, new_len, width), bf16),
            pltpu.VMEM((1, local, total, HEAD_SIZE), bf16),
            pltpu.VMEM((1, local, total, HEAD_SIZE), bf16),
        ),
        in_specs=[in_hbm] * 7,
        out_specs=(vmem,) * 5,
        scratch_shapes=[
            pltpu.VMEM((n * KEEP, count, rows, HEAD_SIZE), bf16)
            for _, _, count in chunks
        ]
        + [
            pltpu.VMEM((heads, plane, KEEP, 2, rows, HEAD_SIZE), bf16),
            pltpu.VMEM((heads, plane * local, 2, rows, HEAD_SIZE), bf16),
            pltpu.VMEM((heads, plane * local, 2, rows, HEAD_SIZE), bf16),
            pltpu.VMEM((heads, local, 2, step_len, HEAD_SIZE), bf16),
            pltpu.VMEM((front, local, new_len, width), bf16),
            pltpu.VMEM((front, local, total, HEAD_SIZE), bf16),
            pltpu.VMEM((front, local, total, HEAD_SIZE), bf16),
            pltpu.VMEM((n, local, 128), jnp.float32),
            pltpu.VMEM(row.shape, jnp.int32),
            pltpu.VMEM(prm_last.shape, bf16),
            pltpu.VMEM((1, value_head.shape[0]), jnp.float32),
            pltpu.VMEM(step_kv.shape, bf16),
            pltpu.VMEM(row.shape, jnp.int32),
            pltpu.SMEM(row.shape, jnp.int32),
            pltpu.SMEM(row.shape, jnp.int32),
            dma((n,)), dma((n,)),
            dma((many, plane)), dma((many, plane)),
            dma((many, 2)), dma((many, nz)),
            dma((2, plane)), dma((nz, plane)),
            dma((many, plane)),
            dma((many, plane)), dma((many, plane)),
            dma((heads, 5)), dma((6,)),
        ],
        compiler_params=pltpu.CompilerParams(
            collective_id=0, has_side_effects=True, vmem_limit_bytes=44 << 20
        ),
    )(
        *(
            pltpu.with_memory_space_constraint(x, pltpu.HBM)
            for x in (row, prm_last, value_head.reshape(1, -1), step_kv)
        ),
        queries, new_keys, new_values,
    )
    return pl.pallas_call(
        close_kernel,
        out_shape=(
            jax.ShapeDtypeStruct(queries.shape, bf16),
            jax.ShapeDtypeStruct((local,), jnp.float32),
        ),
        in_specs=[vmem] * 5,
        out_specs=(anywhere, smem),
        scratch_shapes=[
            pltpu.VMEM((1, local, new_len, width), bf16),
            dma((front,)), dma((local,)),
        ],
        compiler_params=pltpu.CompilerParams(vmem_limit_bytes=24 << 20),
    )(shares, part, qlast, klast, vlast)


def line_body(queries, new_keys, new_values, step_kv, prm_last, value_head, parents):
    n = lax.axis_size("beam")
    ny = 1
    nz = n // (2 * ny)
    me = lax.axis_index("beam")
    local, new_len, qwidth = queries.shape
    children = parents.shape[0]
    step_len, kv_width = step_kv.shape[2:]
    heads = kv_width // HEAD_SIZE
    width = qwidth // heads

    beams = jnp.arange(n * local, dtype=jnp.int32)
    equal = parents[None, :] == beams[:, None]
    hits = jnp.sum(equal.astype(jnp.int32), axis=1)
    kept = (hits > 0).astype(jnp.int32)
    before = jnp.sum(kept[None, :] * (beams[None, :] < beams[:, None]), axis=1)
    rank_of_beam = before % KEEP
    wanted = (
        (beams[None, :] // local == me)
        & (kept[None, :] > 0)
        & (rank_of_beam[None, :] == jnp.arange(KEEP, dtype=jnp.int32)[:, None])
    )
    keep_pos = jnp.sum(wanted * (beams % local)[None, :], axis=1).astype(jnp.int32)
    rank = jnp.sum(equal * rank_of_beam[:, None], axis=0)
    owner = parents // local
    c, y, z = owner % 2, (owner // 2) % ny, owner // (2 * ny)
    my_c, my_y = me % 2, (me // 2) % ny
    code = jnp.where(y == my_y, ((c != my_c) * nz + z) * KEEP + rank, -1).astype(jnp.int32)
    y_peer = me + 2 - 4 * my_y if ny > 1 else me
    own = lax.dynamic_slice_in_dim(code, me * local, local)
    other = lax.dynamic_slice_in_dim(code, y_peer * local, local)
    idx = jnp.concatenate([keep_pos, own, other])

    dma = pltpu.SemaphoreType.DMA
    bf16 = jnp.bfloat16
    vmem = pl.BlockSpec(memory_space=pltpu.VMEM)
    anywhere = pl.BlockSpec(memory_space=pl.ANY)
    last = 2
    front = heads - last
    part, rewards, tail = pl.pallas_call(
        functools.partial(kernel, n, ny, nz),
        out_shape=(
            jax.ShapeDtypeStruct((local, new_len, front * width), bf16),
            jax.ShapeDtypeStruct((n, local, 128), jnp.float32),
            jax.ShapeDtypeStruct((last, local, 2, step_len, HEAD_SIZE), bf16),
        ),
        in_specs=[pl.BlockSpec(memory_space=pltpu.SMEM), vmem, vmem, vmem]
        + [anywhere] * 3,
        out_specs=(anywhere, vmem, vmem),
        scratch_shapes=[
            pltpu.VMEM((heads, 2, nz, KEEP, 2, step_len, HEAD_SIZE), bf16),
            pltpu.VMEM((heads, local, 2, step_len, HEAD_SIZE), bf16),
            pltpu.VMEM((heads, local, 2, step_len, HEAD_SIZE), bf16),
            pltpu.VMEM((front, local, new_len, width), bf16),
            pltpu.VMEM((front, local, new_len + step_len, HEAD_SIZE), bf16),
            pltpu.VMEM((front, local, new_len + step_len, HEAD_SIZE), bf16),
            pltpu.VMEM((front, local, new_len, width), bf16),
            dma((n,)), dma((n,)),
            dma((heads, nz)), dma((heads, nz)), dma((heads,)),
            dma((heads,)), dma((heads,)),
            dma((heads,)), dma((heads,)),
            dma((front, 5)), dma((front,)),
        ],
        compiler_params=pltpu.CompilerParams(
            collective_id=0, has_side_effects=True, vmem_limit_bytes=56 << 20
        ),
    )(idx, prm_last, value_head.reshape(1, -1), step_kv, queries, new_keys, new_values)

    attended = pl.pallas_call(
        functools.partial(last_kernel, front),
        out_shape=jax.ShapeDtypeStruct(queries.shape, bf16),
        in_specs=[vmem] + [anywhere] * 4,
        out_specs=anywhere,
        scratch_shapes=[
            pltpu.VMEM((last, local, new_len, width), bf16),
            pltpu.VMEM((last, local, new_len + step_len, HEAD_SIZE), bf16),
            pltpu.VMEM((last, local, new_len + step_len, HEAD_SIZE), bf16),
            pltpu.VMEM((last, local, new_len, width), bf16),
            pltpu.VMEM((local, new_len, front * width), bf16),
            dma((last, 5)), dma((last,)), dma((local,)), dma((local,)),
        ],
        compiler_params=pltpu.CompilerParams(vmem_limit_bytes=56 << 20),
    )(tail, part, queries, new_keys, new_values)

    reward = rewards[:, :, 0].reshape(-1)
    total = jnp.sum(reward * hits.astype(jnp.float32))
    mine = lax.dynamic_slice_in_dim(parents, me * local, local)
    match = mine[:, None] == beams[None, :]
    child_reward = jnp.sum(jnp.where(match, reward[None, :], 0.0), axis=1)
    child_share = children * child_reward / total
    return (attended, child_share)


def solution(mesh):
    in_specs = (
        P(("prompts", "beam"), None, None),
        P(("prompts", "beam"), None, None),
        P(("prompts", "beam"), None, None),
        P(("prompts", "beam"), None, None, None),
        P(("prompts", "beam"), None),
        P(),
        P("prompts"),
    )
    out_specs = (P(("prompts", "beam"), None, None), P(("prompts", "beam")))
    body = plane_body if mesh.shape["beam"] == 16 else line_body
    return jax.shard_map(body, mesh=mesh, in_specs=in_specs, out_specs=out_specs, check_vma=False)
```

```python
import functools

import jax
import jax.numpy as jnp
from jax import lax
from jax.experimental import pallas as pl
from jax.experimental.pallas import tpu as pltpu
from jax.sharding import PartitionSpec as P

HEAD_SIZE = 128
KEEP = 2
LOG2E = 1.4426950408889634


def remote(src, dst, send, recv, device):
    return pltpu.make_async_remote_copy(
        src_ref=src, dst_ref=dst, send_sem=send, recv_sem=recv,
        device_id={"beam": device}, device_id_type=pl.DeviceIdType.MESH,
    )


def loads(k, head, hbm, buf, isem):
    q_hbm, nk_hbm, nv_hbm = hbm
    qbuf, kbuf, vbuf, _ = buf
    width = qbuf.shape[3]
    half = q_hbm.shape[1] // 2
    cols = pl.ds(pl.multiple_of(head * HEAD_SIZE, HEAD_SIZE), HEAD_SIZE)
    wide = pl.ds(pl.multiple_of(head * width, width), width)
    lo, hi = pl.ds(0, half), pl.ds(half, half)
    return [
        pltpu.make_async_copy(q_hbm.at[:, :, wide], qbuf.at[k], isem.at[k, 0]),
        pltpu.make_async_copy(nk_hbm.at[:, hi, cols], kbuf.at[k, :, lo], isem.at[k, 1]),
        pltpu.make_async_copy(nk_hbm.at[:, lo, cols], kbuf.at[k, :, hi], isem.at[k, 2]),
        pltpu.make_async_copy(nv_hbm.at[:, hi, cols], vbuf.at[k, :, lo], isem.at[k, 3]),
        pltpu.make_async_copy(nv_hbm.at[:, lo, cols], vbuf.at[k, :, hi], isem.at[k, 4]),
    ]


def store(k, head, obuf, out_hbm, osem):
    width = obuf.shape[3]
    wide = pl.ds(pl.multiple_of(head * width, width), width)
    return pltpu.make_async_copy(obuf.at[k], out_hbm.at[:, :, wide], osem.at[k])


def attend(k, j, buf):
    qbuf, kbuf, vbuf, obuf = buf
    half = qbuf.shape[2] // 2
    group = qbuf.shape[3] // HEAD_SIZE
    row = lax.rem(lax.broadcasted_iota(jnp.int32, (group * half, half), 0), half)
    column = lax.broadcasted_iota(jnp.int32, (group * half, half), 1)
    visible = column <= row
    scale = HEAD_SIZE ** (-0.5) * LOG2E
    for part in range(2):
        start = half if part == 0 else 0
        keys = kbuf[k, j, start:]
        values = vbuf[k, j, start:]
        values = jnp.concatenate([values, jnp.ones_like(values)], axis=1)
        rows = slice(part * half, (part + 1) * half)
        query = jnp.concatenate(
            [qbuf[k, j, rows, g * HEAD_SIZE:(g + 1) * HEAD_SIZE] for g in range(group)],
            axis=0,
        )
        s = lax.dot_general(
            query, keys, (((1,), (1,)), ((), ())), preferred_element_type=jnp.float32
        )
        s = jnp.concatenate(
            [jnp.where(visible, s[:, :half], -jnp.inf), s[:, half:]], axis=1
        )
        top = jnp.max(s, axis=1, keepdims=True)
        p = jnp.exp2((s - top) * scale).astype(jnp.bfloat16)
        o = jnp.dot(p, values, preferred_element_type=jnp.float32)
        o = (o[:, :HEAD_SIZE] / o[:, HEAD_SIZE:]).astype(jnp.bfloat16)
        for g in range(group):
            obuf[k, j, rows, g * HEAD_SIZE:(g + 1) * HEAD_SIZE] = o[
                g * half:(g + 1) * half
            ]


def last_kernel(
    first, tail, part, q_hbm, nk_hbm, nv_hbm, out_hbm,
    qbuf, kbuf, vbuf, obuf, held, isem, osem, hin, hout,
):
    hbm = (q_hbm, nk_hbm, nv_hbm)
    buf = (qbuf, kbuf, vbuf, obuf)
    local, new_len, done = held.shape
    count = qbuf.shape[0]

    def fetch(j):
        return pltpu.make_async_copy(part.at[j], held.at[j], hin.at[j])

    def put(j):
        return pltpu.make_async_copy(
            held.at[j], out_hbm.at[j, :, pl.ds(0, done)], hout.at[j]
        )

    for k in range(count):
        for copy in loads(k, first + k, hbm, buf, isem):
            copy.start()
        if k == 0:
            for j in range(local):
                fetch(j).start()
    for k in range(count):
        for j in range(local):
            kbuf[k, j, new_len:] = tail[k, j, 0]
            vbuf[k, j, new_len:] = tail[k, j, 1]
    for k in range(count):
        for copy in loads(k, first + k, hbm, buf, isem):
            copy.wait()
        if k > 0:
            for j in range(local):
                fetch(j).wait()
                put(j).start()

        def one(j, carry):
            attend(k, j, buf)
            return carry

        lax.fori_loop(0, local, one, 0, unroll=2)
        store(k, first + k, obuf, out_hbm, osem).start()
    for j in range(local):
        put(j).wait()
    for k in range(count):
        store(k, first + k, obuf, out_hbm, osem).wait()


def kernel(
    n, ny, nz, idx, prm, head, kv, q_hbm, nk_hbm, nv_hbm, out_hbm, rbuf, tail,
    col, pbuf, ybuf, qbuf, kbuf, vbuf, obuf,
    rsend, rrecv, zsend, zrecv, lsend, csend, crecv, ysend, yrecv, isem, osem,
):
    me = lax.axis_index("beam")
    my_c = lax.rem(me, 2)
    my_y = lax.rem(lax.div(me, 2), ny)
    my_z = lax.div(me, 2 * ny)
    local = kv.shape[0]
    step_len = kv.shape[2]
    heads = kv.shape[3] // HEAD_SIZE
    new_len = q_hbm.shape[1]
    front = qbuf.shape[0]
    hbm = (q_hbm, nk_hbm, nv_hbm)
    buf = (qbuf, kbuf, vbuf, obuf)

    def at(z, y, c):
        return (z * ny + y) * 2 + c

    core_peer = at(my_z, my_y, 1 - my_c)
    y_peer = at(my_z, lax.rem(my_y + 1, ny), my_c)

    barrier = pltpu.get_barrier_semaphore()

    def greet(d, carry):
        pl.semaphore_signal(
            barrier, inc=1, device_id={"beam": lax.rem(me + d, n)},
            device_id_type=pl.DeviceIdType.MESH,
        )
        return carry

    lax.fori_loop(1, n, greet, 0)

    def load(k, carry):
        for copy in loads(k, k, hbm, buf, isem):
            copy.start()
        return carry

    lax.fori_loop(0, front, load, 0)

    for k in range(heads):
        cols = slice(k * HEAD_SIZE, (k + 1) * HEAD_SIZE)
        for r in range(KEEP):
            tile = kv[0, :, :, cols]
            for b in range(1, local):
                tile = jnp.where(idx[r] == b, kv[b, :, :, cols], tile)
            col[k, 0, my_z, r] = tile

    hidden = prm[...].astype(jnp.float32)
    square = jnp.mean(hidden * hidden, axis=-1, keepdims=True)
    normed = hidden * lax.rsqrt(square + 1e-05)
    score = jnp.sum(normed * head[...], axis=-1, keepdims=True)
    reward = (1.0 / (1.0 + jnp.exp(-score))).astype(jnp.bfloat16).astype(jnp.float32)
    rbuf[me] = jnp.broadcast_to(reward, (local, 128))

    pl.semaphore_wait(barrier, n - 1)

    def z_copy(k, d):
        zt = lax.rem(my_z + d, nz)
        return remote(
            col.at[k, 0, my_z], col.at[k, 0, my_z],
            zsend.at[k, d], zrecv.at[k, my_z], at(zt, my_y, my_c),
        )

    def z_arrival(k, d):
        zs = lax.rem(my_z + d, nz)
        return remote(
            col.at[k, 0, zs], col.at[k, 0, zs],
            zsend.at[k, d], zrecv.at[k, zs], at(zs, my_y, my_c),
        )

    relayed = nz == 4

    def when_direct(d, run):
        if relayed and d == 1:
            pl.when(my_z != nz - 1)(run)
        elif relayed and d == nz - 1:
            pl.when(my_z != 0)(run)
        else:
            run()

    def relay_copy(k, source, target):
        return remote(
            col.at[k, 0, source], col.at[k, 0, source],
            lsend.at[k], zrecv.at[k, source], at(target, my_y, my_c),
        )

    ends = ((nz - 2, 0, nz - 1), (1, nz - 1, 0)) if relayed else ()

    def relay(k):
        for who, source, target in ends:

            @pl.when(my_z == who)
            def _():
                relay_copy(k, source, target).wait_recv()
                relay_copy(k, source, target).start()

    def z_wait(k):
        for d in range(1, nz):
            zs = lax.rem(my_z + d, nz)
            got = (my_z == 1) & (zs == nz - 1) | (my_z == nz - 2) & (zs == 0)
            if relayed:

                @pl.when(jnp.logical_not(got))
                def _():
                    z_arrival(k, d).wait_recv()
            else:
                z_arrival(k, d).wait_recv()

    def z_start(k, carry):
        for d in range(1, nz):
            when_direct(d, z_copy(k, d).start)
        return carry

    def r_copy(d):
        return remote(rbuf.at[me], rbuf.at[me], rsend.at[d], rrecv.at[me], lax.rem(me + d, n))

    def r_arrival(d):
        src = lax.rem(me + d, n)
        return remote(rbuf.at[src], rbuf.at[src], rsend.at[d], rrecv.at[src], src)

    lax.fori_loop(0, heads, z_start, 0)

    def r_start(d, carry):
        r_copy(d).start()
        return carry

    lax.fori_loop(1, n, r_start, 0)

    def c_copy(k):
        return remote(col.at[k, 0], col.at[k, 1], csend.at[k], crecv.at[k], core_peer)

    def y_copy(k):
        return remote(pbuf.at[k], ybuf.at[k], ysend.at[k], yrecv.at[k], y_peer)

    def pick(k, codes, bases):
        tiles = list(bases)
        for c in range(2):
            for z in range(nz):
                for r in range(KEEP):
                    entry = col[k, c, z, r]
                    slot = (c * nz + z) * KEEP + r
                    tiles = [
                        jnp.where(code == slot, entry, tile)
                        for code, tile in zip(codes, tiles)
                    ]
        return tiles

    def exchange_one(k):
        z_wait(k)
        c_copy(k).start()

    def exchange_two(k):
        c_copy(k).wait_recv()
        if ny > 1:
            codes = [idx[KEEP + local + j] for j in range(local)]
            tiles = pick(k, codes, [col[k, 0, 0, 0]] * local)
            for j in range(local):
                pbuf[k, j] = tiles[j]
            y_copy(k).start()

    def parents_of(k):
        if ny > 1:
            y_copy(k).wait_recv()
        bases = [ybuf[k, j] if ny > 1 else col[k, 0, 0, 0] for j in range(local)]
        return pick(k, [idx[KEEP + j] for j in range(local)], bases)

    def place(k):
        tiles = parents_of(k)
        for j in range(local):
            kbuf[k, j, new_len:] = tiles[j][0]
            vbuf[k, j, new_len:] = tiles[j][1]

    def attend_some(k, first, last):
        def one(j, carry):
            attend(k, j, buf)
            return carry

        lax.fori_loop(first, last, one, 0, unroll=True)

    def ready(k):
        for copy in loads(k, k, hbm, buf, isem):
            copy.wait()
        place(k)

    def finish_head(k):
        attend_some(k, local // 2, local)
        store(k, k, obuf, out_hbm, osem).start()

    def start_head(k):
        ready(k)
        attend_some(k, 0, local // 2)

    relay(0)
    exchange_one(0)
    relay(1)
    exchange_one(1)
    exchange_two(0)
    relay(2)

    def step(k, carry):
        exchange_one(k)
        exchange_two(k - 1)
        pl.when(k + 1 < heads)(functools.partial(relay, k + 1))
        start_head(k - 2)
        finish_head(k - 2)
        return carry

    lax.fori_loop(2, heads, step, 0)
    exchange_two(heads - 1)
    for k in range(front, heads):
        tiles = parents_of(k)
        for j in range(local):
            tail[k - front, j] = tiles[j]

    def finish(k, carry):
        for d in range(1, nz):
            when_direct(d, z_copy(k, d).wait_send)
        for who, source, target in ends:
            pl.when(my_z == who)(relay_copy(k, source, target).wait_send)
        c_copy(k).wait_send()
        if ny > 1:
            y_copy(k).wait_send()
        return carry

    lax.fori_loop(0, heads, finish, 0)

    def stored(k, carry):
        store(k, k, obuf, out_hbm, osem).wait()
        return carry

    lax.fori_loop(0, front, stored, 0)

    def r_finish(d, carry):
        r_arrival(d).wait_recv()
        r_copy(d).wait_send()
        return carry

    lax.fori_loop(1, n, r_finish, 0)


def halves(heads):
    return [(k, 0, 2) for k in range(heads)]


def plane_kernel(
    nz, row_hbm, prm_hbm, head_hbm, kv_hbm, q_hbm, nk_hbm, nv_hbm,
    obuf, shares, qlast, klast, vlast, *scratch
):
    local, _, step_len, kv_width = kv_hbm.shape
    heads = kv_width // HEAD_SIZE
    chunks = halves(heads)
    raws = scratch[:len(chunks)]
    (
        kept, picked, share, held, qbuf, kbuf, vbuf, rbuf,
        row, prm, head, kv, crow, listed, code,
        rsend, rrecv, asend, arecv, zsend, zrecv, fsend, frecv, psend,
        msend, mrecv, isem, csem,
    ) = scratch[len(chunks):]
    me = lax.axis_index("beam")
    plane = kept.shape[1]
    n = nz * plane
    rows = step_len // plane
    new_len = q_hbm.shape[1]
    front = qbuf.shape[0]
    hbm = (q_hbm, nk_hbm, nv_hbm)
    buf = (qbuf, kbuf, vbuf, obuf)
    my_q = lax.rem(me, plane)
    my_z = lax.div(me, plane)
    inner = (my_z == 1) | (my_z == 2)
    outer = jnp.logical_not(inner)
    near = jnp.where(my_z < 2, 1 - my_z, 5 - my_z)
    my_rows = pl.ds(pl.multiple_of(my_q * rows, rows), rows)

    inputs = [
        pltpu.make_async_copy(src, dst, csem.at[i])
        for i, (src, dst) in enumerate(
            [(row_hbm, listed), (kv_hbm, kv), (row_hbm, row), (prm_hbm, prm), (head_hbm, head)]
        )
    ]
    for copy in inputs:
        copy.start()

    barrier = pltpu.get_barrier_semaphore()

    def greet(d, carry):
        pl.semaphore_signal(
            barrier, inc=1, device_id={"beam": lax.rem(me + d, n)},
            device_id_type=pl.DeviceIdType.MESH,
        )
        return carry

    lax.fori_loop(1, n, greet, 0)

    inputs[0].wait()
    low, high = local - 1, 0
    for c in range(listed.shape[1]):
        spot = listed[0, c] - me * local
        mine = (spot >= 0) & (spot < local)
        low = jnp.where(mine, jnp.minimum(low, spot), low)
        high = jnp.where(mine, jnp.maximum(high, spot), high)
    inputs[1].wait()

    def keep(c):
        k, lo, count = chunks[c]
        cols = slice(k * HEAD_SIZE, (k + 1) * HEAD_SIZE)
        part = slice(lo, lo + count)
        for r, beam in enumerate((low, high)):
            raws[c][me * KEEP + r] = kv[beam, part, my_rows, cols]
            for q in range(plane):
                kept[k, q, r, part] = kv[beam, part, q * rows:(q + 1) * rows, cols]

    keep(0)
    pl.semaphore_wait(barrier, n - 1)

    def mate(d):
        if d == 1:
            return my_q + 1 - 2 * lax.rem(my_q, 2)
        return lax.rem(my_q + 2, plane) if d == 2 else plane - 1 - my_q

    def a_part(c, q, source):
        k, lo, count = chunks[c]
        slot = pl.ds((my_z * plane + source) * KEEP, KEEP)
        return kept.at[k, q, :, pl.ds(lo, count)], raws[c].at[slot]

    def a_copy(c, d):
        src, dst = a_part(c, mate(d), my_q)
        return remote(
            src, dst, asend.at[c, d], arecv.at[c, my_q], my_z * plane + mate(d)
        )

    def a_arrival(c, d):
        src, dst = a_part(c, mate(d), mate(d))
        return remote(
            src, dst, asend.at[c, d], arecv.at[c, mate(d)], my_z * plane + mate(d)
        )

    def z_copy(c, i, target):
        slot = pl.ds(my_z * plane * KEEP, plane * KEEP)
        return remote(
            raws[c].at[slot], raws[c].at[slot], zsend.at[c, i], zrecv.at[c, my_z],
            target * plane + my_q,
        )

    def z_arrival(c, d):
        z = lax.rem(my_z + d, nz)
        slot = pl.ds(z * plane * KEEP, plane * KEEP)
        return remote(
            raws[c].at[slot], raws[c].at[slot], zsend.at[c, 0], zrecv.at[c, z],
            z * plane + my_q,
        )

    def f_copy(q, i, target):
        slot = pl.ds((my_z * plane + q) * KEEP, KEEP)
        return remote(
            raws[0].at[slot], raws[0].at[slot], fsend.at[i, q], frecv.at[my_z, q],
            target * plane + my_q,
        )

    def f_arrival(d, q):
        z = lax.rem(my_z + d, nz)
        slot = pl.ds((z * plane + q) * KEEP, KEEP)
        return remote(
            raws[0].at[slot], raws[0].at[slot], fsend.at[0, q], frecv.at[z, q],
            z * plane + my_q,
        )

    def along(do):
        @pl.when(outer)
        def _():
            do(0, nz - 1 - near)
            do(1, near)

        @pl.when(inner)
        def _():
            do(0, nz - 1 - my_z)

    def slices(c, source):
        k, lo, count = chunks[c]
        part = pl.ds(lo, count)
        return k, part, held.at[k, source, :, part]

    def p_copy(c, q):
        k, part, dst = slices(c, my_q)
        return remote(
            picked.at[k, pl.ds(q * local, local), part], dst,
            psend.at[c, q], mrecv.at[c, my_q], near * plane + q,
        )

    def p_arrival(c, q):
        k, part, dst = slices(c, q)
        return remote(
            picked.at[k, pl.ds(q * local, local), part], dst,
            psend.at[c, q], mrecv.at[c, q], near * plane + q,
        )

    def m_copy(c, d):
        k, part, dst = slices(c, my_q)
        q = mate(d)
        return remote(
            share.at[k, pl.ds(q * local, local), part], dst,
            msend.at[c, d], mrecv.at[c, my_q], my_z * plane + q,
        )

    def m_arrival(c, d):
        q = mate(d)
        k, part, dst = slices(c, q)
        return remote(
            share.at[k, pl.ds(q * local, local), part], dst,
            msend.at[c, d], mrecv.at[c, q], my_z * plane + q,
        )

    def r_copy(d):
        return remote(rbuf.at[me], rbuf.at[me], rsend.at[d], rrecv.at[me], lax.rem(me + d, n))

    def r_arrival(d):
        src = lax.rem(me + d, n)
        return remote(rbuf.at[src], rbuf.at[src], rsend.at[d], rrecv.at[src], src)

    def a_start(c):
        for d in range(1, plane):
            a_copy(c, d).start()

    along(lambda i, target: f_copy(my_q, i, target).start())
    a_start(0)
    for c in range(1, len(chunks)):
        keep(c)
        a_start(c)
    for d in range(1, plane):
        a_arrival(0, d).wait_recv()
        along(lambda i, target: f_copy(mate(d), i, target).start())
    for c in range(1, len(chunks)):
        for d in range(1, plane):
            a_arrival(c, d).wait_recv()
        along(lambda i, target: z_copy(c, i, target).start())

    inputs[2].wait()
    ids = row[...]
    owner = lax.div(ids, local)
    groups = lax.broadcasted_iota(jnp.int32, (n, ids.shape[1]), 0)
    own = groups == owner
    first = jnp.min(jnp.where(own, ids, n * local), axis=1, keepdims=True)
    first = jnp.min(jnp.where(own, first, n * local), axis=0, keepdims=True)
    crow[...] = owner * KEEP + (ids > first).astype(jnp.int32)
    numbers = pltpu.make_async_copy(crow, code, csem.at[len(inputs)])
    numbers.start()

    def last_loads():
        return loads(0, heads - 1, hbm, (qlast, klast, vlast, None), isem.at[pl.ds(front, 1)])

    def load(k, carry):
        for copy in loads(k, k, hbm, buf, isem):
            copy.start()
        return carry

    lax.fori_loop(0, front, load, 0)
    for copy in last_loads():
        copy.start()

    inputs[3].wait()
    inputs[4].wait()
    hidden = prm[...].astype(jnp.float32)
    square = jnp.mean(hidden * hidden, axis=-1, keepdims=True)
    normed = hidden * lax.rsqrt(square + 1e-05)
    score = jnp.sum(normed * head[...], axis=-1, keepdims=True)
    reward = (1.0 / (1.0 + jnp.exp(-score))).astype(jnp.bfloat16).astype(jnp.float32)
    rbuf[me] = jnp.broadcast_to(reward, (local, 128))

    def r_start(d, carry):
        r_copy(d).start()
        return carry

    lax.fori_loop(1, n, r_start, 0)
    numbers.wait()

    def pass_on(c):
        k, lo, count = chunks[c]
        part = slice(lo, lo + count)

        @pl.when(inner)
        def _():
            for d in range(1, nz):
                if c == 0:
                    for q in range(plane):
                        f_arrival(d, q).wait_recv()
                else:
                    z_arrival(c, d).wait_recv()
            for q in range(plane):
                for t in range(q * local, (q + 1) * local):
                    picked[k, t, part] = raws[c][code[0, near * plane * local + t]]
                p_copy(c, q).start()
            for t in range(plane * local):
                share[k, t, part] = raws[c][code[0, my_z * plane * local + t]]
            for d in range(1, plane):
                m_copy(c, d).start()
            held[k, my_q, :, part] = share[k, pl.ds(my_q * local, local), part]

    def arrived(c):
        @pl.when(inner)
        def _():
            for d in range(1, plane):
                m_arrival(c, d).wait_recv()

        @pl.when(outer)
        def _():
            for q in range(plane):
                p_arrival(c, q).wait_recv()

    def place(k, keys, values):
        for j in range(local):
            for q in range(plane):
                span = slice(new_len + q * rows, new_len + (q + 1) * rows)
                keys[j, span] = held[k, q, j, 0]
                values[j, span] = held[k, q, j, 1]

    def begin(k):
        for copy in loads(k, k, hbm, buf, isem):
            copy.wait()
        place(k, kbuf.at[k], vbuf.at[k])

    def attend_some(k, lo, hi):
        def one(j, inside):
            attend(k, j, buf)
            return inside

        lax.fori_loop(lo, hi, one, 0, unroll=True)

    for c in range(2):
        pass_on(c)

    def step(k, carry):
        for c in range(2, heads):
            pl.when(k + 2 == c)(functools.partial(pass_on, c))
        for c in range(front):
            pl.when(k == c)(functools.partial(arrived, c))
        begin(k)
        attend_some(k, 0, local)
        return carry

    lax.fori_loop(0, front, step, 0)

    def r_finish(d, carry):
        r_arrival(d).wait_recv()
        r_copy(d).wait_send()
        return carry

    lax.fori_loop(1, n, r_finish, 0)
    reward = rbuf[:, :, :ids.shape[1]]
    beam = lax.broadcasted_iota(jnp.int32, reward.shape, 0) * local
    beam = beam + lax.broadcasted_iota(jnp.int32, reward.shape, 1)
    given = jnp.where(beam == row[...][None], reward, 0.0)
    given = jnp.sum(jnp.sum(given, axis=0), axis=0, keepdims=True)
    shares[...] = ids.shape[1] * given / jnp.sum(given, axis=1, keepdims=True)

    for copy in last_loads():
        copy.wait()
    arrived(front)
    place(heads - 1, klast.at[0], vlast.at[0])

    along(lambda i, target: [f_copy(q, i, target).wait_send() for q in range(plane)])
    for c in range(len(chunks)):
        for d in range(1, plane):
            a_copy(c, d).wait_send()
        if c > 0:
            along(lambda i, target: z_copy(c, i, target).wait_send())

        @pl.when(inner)
        def _():
            for q in range(plane):
                p_copy(c, q).wait_send()
            for d in range(1, plane):
                m_copy(c, d).wait_send()


def close_kernel(
    shares, part, qlast, klast, vlast, out_hbm, mine, obuf, psem, osem
):
    front, local, _, width = part.shape

    def move(k):
        return pltpu.make_async_copy(
            part.at[k], out_hbm.at[:, :, pl.ds(k * width, width)], psem.at[k]
        )

    def put(j):
        return pltpu.make_async_copy(
            obuf.at[0, j], out_hbm.at[j, :, pl.ds(front * width, width)], osem.at[j]
        )

    for k in range(front):
        move(k).start()
    me = lax.axis_index("beam")
    all_shares = shares[...]
    lane = lax.broadcasted_iota(jnp.int32, all_shares.shape, 1)
    for j in range(local):
        mine[j] = jnp.sum(jnp.where(lane == me * local + j, all_shares, 0.0))
    for j in range(local):
        attend(0, j, (qlast, klast, vlast, obuf))
        put(j).start()
    for k in range(front):
        move(k).wait()
    for j in range(local):
        put(j).wait()


def plane_body(queries, new_keys, new_values, step_kv, prm_last, value_head, parents):
    n = lax.axis_size("beam")
    ny, nz = 2, 4
    plane = 2 * ny
    local, new_len, qwidth = queries.shape
    step_len, kv_width = step_kv.shape[2:]
    heads = kv_width // HEAD_SIZE
    width = qwidth // heads
    rows = step_len // plane
    front = heads - 1
    chunks = halves(heads)
    many = len(chunks)
    total = new_len + step_len
    dma = pltpu.SemaphoreType.DMA
    bf16 = jnp.bfloat16
    vmem = pl.BlockSpec(memory_space=pltpu.VMEM)
    smem = pl.BlockSpec(memory_space=pltpu.SMEM)
    in_hbm = pl.BlockSpec(memory_space=pltpu.HBM)
    anywhere = pl.BlockSpec(memory_space=pl.ANY)
    row = parents.reshape(1, -1)
    part, shares, qlast, klast, vlast = pl.pallas_call(
        functools.partial(plane_kernel, nz),
        out_shape=(
            pltpu.VMEM((front, local, new_len, width), bf16),
            pltpu.VMEM(row.shape, jnp.float32),
            pltpu.VMEM((1, local, new_len, width), bf16),
            pltpu.VMEM((1, local, total, HEAD_SIZE), bf16),
            pltpu.VMEM((1, local, total, HEAD_SIZE), bf16),
        ),
        in_specs=[in_hbm] * 7,
        out_specs=(vmem,) * 5,
        scratch_shapes=[
            pltpu.VMEM((n * KEEP, count, rows, HEAD_SIZE), bf16)
            for _, _, count in chunks
        ]
        + [
            pltpu.VMEM((heads, plane, KEEP, 2, rows, HEAD_SIZE), bf16),
            pltpu.VMEM((heads, plane * local, 2, rows, HEAD_SIZE), bf16),
            pltpu.VMEM((heads, plane * local, 2, rows, HEAD_SIZE), bf16),
            pltpu.VMEM((heads, plane, local, 2, rows, HEAD_SIZE), bf16),
            pltpu.VMEM((front, local, new_len, width), bf16),
            pltpu.VMEM((front, local, total, HEAD_SIZE), bf16),
            pltpu.VMEM((front, local, total, HEAD_SIZE), bf16),
            pltpu.VMEM((n, local, 128), jnp.float32),
            pltpu.VMEM(row.shape, jnp.int32),
            pltpu.VMEM(prm_last.shape, bf16),
            pltpu.VMEM((1, value_head.shape[0]), jnp.float32),
            pltpu.VMEM(step_kv.shape, bf16),
            pltpu.VMEM(row.shape, jnp.int32),
            pltpu.SMEM(row.shape, jnp.int32),
            pltpu.SMEM(row.shape, jnp.int32),
            dma((n,)), dma((n,)),
            dma((many, plane)), dma((many, plane)),
            dma((many, 2)), dma((many, nz)),
            dma((2, plane)), dma((nz, plane)),
            dma((many, plane)),
            dma((many, plane)), dma((many, plane)),
            dma((heads, 5)), dma((6,)),
        ],
        compiler_params=pltpu.CompilerParams(
            collective_id=0, has_side_effects=True, vmem_limit_bytes=44 << 20
        ),
    )(
        *(
            pltpu.with_memory_space_constraint(x, pltpu.HBM)
            for x in (row, prm_last, value_head.reshape(1, -1), step_kv)
        ),
        queries, new_keys, new_values,
    )
    return pl.pallas_call(
        close_kernel,
        out_shape=(
            jax.ShapeDtypeStruct(queries.shape, bf16),
            jax.ShapeDtypeStruct((local,), jnp.float32),
        ),
        in_specs=[vmem] * 5,
        out_specs=(anywhere, smem),
        scratch_shapes=[
            pltpu.VMEM((1, local, new_len, width), bf16),
            dma((front,)), dma((local,)),
        ],
        compiler_params=pltpu.CompilerParams(vmem_limit_bytes=24 << 20),
    )(shares, part, qlast, klast, vlast)


def line_body(queries, new_keys, new_values, step_kv, prm_last, value_head, parents):
    n = lax.axis_size("beam")
    ny = 1
    nz = n // (2 * ny)
    me = lax.axis_index("beam")
    local, new_len, qwidth = queries.shape
    children = parents.shape[0]
    step_len, kv_width = step_kv.shape[2:]
    heads = kv_width // HEAD_SIZE
    width = qwidth // heads

    beams = jnp.arange(n * local, dtype=jnp.int32)
    equal = parents[None, :] == beams[:, None]
    hits = jnp.sum(equal.astype(jnp.int32), axis=1)
    kept = (hits > 0).astype(jnp.int32)
    before = jnp.sum(kept[None, :] * (beams[None, :] < beams[:, None]), axis=1)
    rank_of_beam = before % KEEP
    wanted = (
        (beams[None, :] // local == me)
        & (kept[None, :] > 0)
        & (rank_of_beam[None, :] == jnp.arange(KEEP, dtype=jnp.int32)[:, None])
    )
    keep_pos = jnp.sum(wanted * (beams % local)[None, :], axis=1).astype(jnp.int32)
    rank = jnp.sum(equal * rank_of_beam[:, None], axis=0)
    owner = parents // local
    c, y, z = owner % 2, (owner // 2) % ny, owner // (2 * ny)
    my_c, my_y = me % 2, (me // 2) % ny
    code = jnp.where(y == my_y, ((c != my_c) * nz + z) * KEEP + rank, -1).astype(jnp.int32)
    y_peer = me + 2 - 4 * my_y if ny > 1 else me
    own = lax.dynamic_slice_in_dim(code, me * local, local)
    other = lax.dynamic_slice_in_dim(code, y_peer * local, local)
    idx = jnp.concatenate([keep_pos, own, other])

    dma = pltpu.SemaphoreType.DMA
    bf16 = jnp.bfloat16
    vmem = pl.BlockSpec(memory_space=pltpu.VMEM)
    anywhere = pl.BlockSpec(memory_space=pl.ANY)
    last = 2
    front = heads - last
    part, rewards, tail = pl.pallas_call(
        functools.partial(kernel, n, ny, nz),
        out_shape=(
            jax.ShapeDtypeStruct((local, new_len, front * width), bf16),
            jax.ShapeDtypeStruct((n, local, 128), jnp.float32),
            jax.ShapeDtypeStruct((last, local, 2, step_len, HEAD_SIZE), bf16),
        ),
        in_specs=[pl.BlockSpec(memory_space=pltpu.SMEM), vmem, vmem, vmem]
        + [anywhere] * 3,
        out_specs=(anywhere, vmem, vmem),
        scratch_shapes=[
            pltpu.VMEM((heads, 2, nz, KEEP, 2, step_len, HEAD_SIZE), bf16),
            pltpu.VMEM((heads, local, 2, step_len, HEAD_SIZE), bf16),
            pltpu.VMEM((heads, local, 2, step_len, HEAD_SIZE), bf16),
            pltpu.VMEM((front, local, new_len, width), bf16),
            pltpu.VMEM((front, local, new_len + step_len, HEAD_SIZE), bf16),
            pltpu.VMEM((front, local, new_len + step_len, HEAD_SIZE), bf16),
            pltpu.VMEM((front, local, new_len, width), bf16),
            dma((n,)), dma((n,)),
            dma((heads, nz)), dma((heads, nz)), dma((heads,)),
            dma((heads,)), dma((heads,)),
            dma((heads,)), dma((heads,)),
            dma((front, 5)), dma((front,)),
        ],
        compiler_params=pltpu.CompilerParams(
            collective_id=0, has_side_effects=True, vmem_limit_bytes=56 << 20
        ),
    )(idx, prm_last, value_head.reshape(1, -1), step_kv, queries, new_keys, new_values)

    attended = pl.pallas_call(
        functools.partial(last_kernel, front),
        out_shape=jax.ShapeDtypeStruct(queries.shape, bf16),
        in_specs=[vmem] + [anywhere] * 4,
        out_specs=anywhere,
        scratch_shapes=[
            pltpu.VMEM((last, local, new_len, width), bf16),
            pltpu.VMEM((last, local, new_len + step_len, HEAD_SIZE), bf16),
            pltpu.VMEM((last, local, new_len + step_len, HEAD_SIZE), bf16),
            pltpu.VMEM((last, local, new_len, width), bf16),
            pltpu.VMEM((local, new_len, front * width), bf16),
            dma((last, 5)), dma((last,)), dma((local,)), dma((local,)),
        ],
        compiler_params=pltpu.CompilerParams(vmem_limit_bytes=56 << 20),
    )(tail, part, queries, new_keys, new_values)

    reward = rewards[:, :, 0].reshape(-1)
    total = jnp.sum(reward * hits.astype(jnp.float32))
    mine = lax.dynamic_slice_in_dim(parents, me * local, local)
    match = mine[:, None] == beams[None, :]
    child_reward = jnp.sum(jnp.where(match, reward[None, :], 0.0), axis=1)
    child_share = children * child_reward / total
    return (attended, child_share)


def solution(mesh):
    in_specs = (
        P(("prompts", "beam"), None, None),
        P(("prompts", "beam"), None, None),
        P(("prompts", "beam"), None, None),
        P(("prompts", "beam"), None, None, None),
        P(("prompts", "beam"), None),
        P(),
        P("prompts"),
    )
    out_specs = (P(("prompts", "beam"), None, None), P(("prompts", "beam")))
    body = plane_body if mesh.shape["beam"] == 16 else line_body
    return jax.shard_map(body, mesh=mesh, in_specs=in_specs, out_specs=out_specs, check_vma=False)
```

```python
import functools

import jax
import jax.numpy as jnp
from jax import lax
from jax.experimental import pallas as pl
from jax.experimental.pallas import tpu as pltpu
from jax.sharding import PartitionSpec as P

HEAD_SIZE = 128
KEEP = 2
LOG2E = 1.4426950408889634


def remote(src, dst, send, recv, device):
    return pltpu.make_async_remote_copy(
        src_ref=src, dst_ref=dst, send_sem=send, recv_sem=recv,
        device_id={"beam": device}, device_id_type=pl.DeviceIdType.MESH,
    )


def loads(k, head, hbm, buf, isem):
    q_hbm, nk_hbm, nv_hbm = hbm
    qbuf, kbuf, vbuf, _ = buf
    width = qbuf.shape[3]
    half = q_hbm.shape[1] // 2
    cols = pl.ds(pl.multiple_of(head * HEAD_SIZE, HEAD_SIZE), HEAD_SIZE)
    wide = pl.ds(pl.multiple_of(head * width, width), width)
    lo, hi = pl.ds(0, half), pl.ds(half, half)
    return [
        pltpu.make_async_copy(q_hbm.at[:, :, wide], qbuf.at[k], isem.at[k, 0]),
        pltpu.make_async_copy(nk_hbm.at[:, hi, cols], kbuf.at[k, :, lo], isem.at[k, 1]),
        pltpu.make_async_copy(nk_hbm.at[:, lo, cols], kbuf.at[k, :, hi], isem.at[k, 2]),
        pltpu.make_async_copy(nv_hbm.at[:, hi, cols], vbuf.at[k, :, lo], isem.at[k, 3]),
        pltpu.make_async_copy(nv_hbm.at[:, lo, cols], vbuf.at[k, :, hi], isem.at[k, 4]),
    ]


def store(k, head, obuf, out_hbm, osem):
    width = obuf.shape[3]
    wide = pl.ds(pl.multiple_of(head * width, width), width)
    return pltpu.make_async_copy(obuf.at[k], out_hbm.at[:, :, wide], osem.at[k])


def attend(k, j, buf):
    qbuf, kbuf, vbuf, obuf = buf
    half = qbuf.shape[2] // 2
    group = qbuf.shape[3] // HEAD_SIZE
    row = lax.rem(lax.broadcasted_iota(jnp.int32, (group * half, half), 0), half)
    column = lax.broadcasted_iota(jnp.int32, (group * half, half), 1)
    visible = column <= row
    scale = HEAD_SIZE ** (-0.5) * LOG2E
    for part in range(2):
        start = half if part == 0 else 0
        keys = kbuf[k, j, start:]
        values = vbuf[k, j, start:]
        values = jnp.concatenate([values, jnp.ones_like(values)], axis=1)
        rows = slice(part * half, (part + 1) * half)
        query = jnp.concatenate(
            [qbuf[k, j, rows, g * HEAD_SIZE:(g + 1) * HEAD_SIZE] for g in range(group)],
            axis=0,
        )
        s = lax.dot_general(
            query, keys, (((1,), (1,)), ((), ())), preferred_element_type=jnp.float32
        )
        s = jnp.concatenate(
            [jnp.where(visible, s[:, :half], -jnp.inf), s[:, half:]], axis=1
        )
        top = jnp.max(s, axis=1, keepdims=True)
        p = jnp.exp2((s - top) * scale).astype(jnp.bfloat16)
        o = jnp.dot(p, values, preferred_element_type=jnp.float32)
        o = (o[:, :HEAD_SIZE] / o[:, HEAD_SIZE:]).astype(jnp.bfloat16)
        for g in range(group):
            obuf[k, j, rows, g * HEAD_SIZE:(g + 1) * HEAD_SIZE] = o[
                g * half:(g + 1) * half
            ]


def last_kernel(
    first, tail, part, q_hbm, nk_hbm, nv_hbm, out_hbm,
    qbuf, kbuf, vbuf, obuf, held, isem, osem, hin, hout,
):
    hbm = (q_hbm, nk_hbm, nv_hbm)
    buf = (qbuf, kbuf, vbuf, obuf)
    local, new_len, done = held.shape
    count = qbuf.shape[0]

    def fetch(j):
        return pltpu.make_async_copy(part.at[j], held.at[j], hin.at[j])

    def put(j):
        return pltpu.make_async_copy(
            held.at[j], out_hbm.at[j, :, pl.ds(0, done)], hout.at[j]
        )

    for k in range(count):
        for copy in loads(k, first + k, hbm, buf, isem):
            copy.start()
        if k == 0:
            for j in range(local):
                fetch(j).start()
    for k in range(count):
        for j in range(local):
            kbuf[k, j, new_len:] = tail[k, j, 0]
            vbuf[k, j, new_len:] = tail[k, j, 1]
    for k in range(count):
        for copy in loads(k, first + k, hbm, buf, isem):
            copy.wait()
        if k > 0:
            for j in range(local):
                fetch(j).wait()
                put(j).start()

        def one(j, carry):
            attend(k, j, buf)
            return carry

        lax.fori_loop(0, local, one, 0, unroll=2)
        store(k, first + k, obuf, out_hbm, osem).start()
    for j in range(local):
        put(j).wait()
    for k in range(count):
        store(k, first + k, obuf, out_hbm, osem).wait()


def kernel(
    n, ny, nz, idx, prm, head, kv, q_hbm, nk_hbm, nv_hbm, out_hbm, rbuf, tail,
    col, pbuf, ybuf, qbuf, kbuf, vbuf, obuf,
    rsend, rrecv, zsend, zrecv, lsend, csend, crecv, ysend, yrecv, isem, osem,
):
    me = lax.axis_index("beam")
    my_c = lax.rem(me, 2)
    my_y = lax.rem(lax.div(me, 2), ny)
    my_z = lax.div(me, 2 * ny)
    local = kv.shape[0]
    step_len = kv.shape[2]
    heads = kv.shape[3] // HEAD_SIZE
    new_len = q_hbm.shape[1]
    front = qbuf.shape[0]
    hbm = (q_hbm, nk_hbm, nv_hbm)
    buf = (qbuf, kbuf, vbuf, obuf)

    def at(z, y, c):
        return (z * ny + y) * 2 + c

    core_peer = at(my_z, my_y, 1 - my_c)
    y_peer = at(my_z, lax.rem(my_y + 1, ny), my_c)

    barrier = pltpu.get_barrier_semaphore()

    def greet(d, carry):
        pl.semaphore_signal(
            barrier, inc=1, device_id={"beam": lax.rem(me + d, n)},
            device_id_type=pl.DeviceIdType.MESH,
        )
        return carry

    lax.fori_loop(1, n, greet, 0)

    def load(k, carry):
        for copy in loads(k, k, hbm, buf, isem):
            copy.start()
        return carry

    lax.fori_loop(0, front, load, 0)

    for k in range(heads):
        cols = slice(k * HEAD_SIZE, (k + 1) * HEAD_SIZE)
        for r in range(KEEP):
            tile = kv[0, :, :, cols]
            for b in range(1, local):
                tile = jnp.where(idx[r] == b, kv[b, :, :, cols], tile)
            col[k, 0, my_z, r] = tile

    hidden = prm[...].astype(jnp.float32)
    square = jnp.mean(hidden * hidden, axis=-1, keepdims=True)
    normed = hidden * lax.rsqrt(square + 1e-05)
    score = jnp.sum(normed * head[...], axis=-1, keepdims=True)
    reward = (1.0 / (1.0 + jnp.exp(-score))).astype(jnp.bfloat16).astype(jnp.float32)
    rbuf[me] = jnp.broadcast_to(reward, (local, 128))

    pl.semaphore_wait(barrier, n - 1)

    def z_copy(k, d):
        zt = lax.rem(my_z + d, nz)
        return remote(
            col.at[k, 0, my_z], col.at[k, 0, my_z],
            zsend.at[k, d], zrecv.at[k, my_z], at(zt, my_y, my_c),
        )

    def z_arrival(k, d):
        zs = lax.rem(my_z + d, nz)
        return remote(
            col.at[k, 0, zs], col.at[k, 0, zs],
            zsend.at[k, d], zrecv.at[k, zs], at(zs, my_y, my_c),
        )

    relayed = nz == 4

    def when_direct(d, run):
        if relayed and d == 1:
            pl.when(my_z != nz - 1)(run)
        elif relayed and d == nz - 1:
            pl.when(my_z != 0)(run)
        else:
            run()

    def relay_copy(k, source, target):
        return remote(
            col.at[k, 0, source], col.at[k, 0, source],
            lsend.at[k], zrecv.at[k, source], at(target, my_y, my_c),
        )

    ends = ((nz - 2, 0, nz - 1), (1, nz - 1, 0)) if relayed else ()

    def relay(k):
        for who, source, target in ends:

            @pl.when(my_z == who)
            def _():
                relay_copy(k, source, target).wait_recv()
                relay_copy(k, source, target).start()

    def z_wait(k):
        for d in range(1, nz):
            zs = lax.rem(my_z + d, nz)
            got = (my_z == 1) & (zs == nz - 1) | (my_z == nz - 2) & (zs == 0)
            if relayed:

                @pl.when(jnp.logical_not(got))
                def _():
                    z_arrival(k, d).wait_recv()
            else:
                z_arrival(k, d).wait_recv()

    def z_start(k, carry):
        for d in range(1, nz):
            when_direct(d, z_copy(k, d).start)
        return carry

    def r_copy(d):
        return remote(rbuf.at[me], rbuf.at[me], rsend.at[d], rrecv.at[me], lax.rem(me + d, n))

    def r_arrival(d):
        src = lax.rem(me + d, n)
        return remote(rbuf.at[src], rbuf.at[src], rsend.at[d], rrecv.at[src], src)

    lax.fori_loop(0, heads, z_start, 0)

    def r_start(d, carry):
        r_copy(d).start()
        return carry

    lax.fori_loop(1, n, r_start, 0)

    def c_copy(k):
        return remote(col.at[k, 0], col.at[k, 1], csend.at[k], crecv.at[k], core_peer)

    def y_copy(k):
        return remote(pbuf.at[k], ybuf.at[k], ysend.at[k], yrecv.at[k], y_peer)

    def pick(k, codes, bases):
        tiles = list(bases)
        for c in range(2):
            for z in range(nz):
                for r in range(KEEP):
                    entry = col[k, c, z, r]
                    slot = (c * nz + z) * KEEP + r
                    tiles = [
                        jnp.where(code == slot, entry, tile)
                        for code, tile in zip(codes, tiles)
                    ]
        return tiles

    def exchange_one(k):
        z_wait(k)
        c_copy(k).start()

    def exchange_two(k):
        c_copy(k).wait_recv()
        if ny > 1:
            codes = [idx[KEEP + local + j] for j in range(local)]
            tiles = pick(k, codes, [col[k, 0, 0, 0]] * local)
            for j in range(local):
                pbuf[k, j] = tiles[j]
            y_copy(k).start()

    def parents_of(k):
        if ny > 1:
            y_copy(k).wait_recv()
        bases = [ybuf[k, j] if ny > 1 else col[k, 0, 0, 0] for j in range(local)]
        return pick(k, [idx[KEEP + j] for j in range(local)], bases)

    def place(k):
        tiles = parents_of(k)
        for j in range(local):
            kbuf[k, j, new_len:] = tiles[j][0]
            vbuf[k, j, new_len:] = tiles[j][1]

    def attend_some(k, first, last):
        def one(j, carry):
            attend(k, j, buf)
            return carry

        lax.fori_loop(first, last, one, 0, unroll=True)

    def ready(k):
        for copy in loads(k, k, hbm, buf, isem):
            copy.wait()
        place(k)

    def finish_head(k):
        attend_some(k, local // 2, local)
        store(k, k, obuf, out_hbm, osem).start()

    def start_head(k):
        ready(k)
        attend_some(k, 0, local // 2)

    relay(0)
    exchange_one(0)
    relay(1)
    exchange_one(1)
    exchange_two(0)
    relay(2)

    def step(k, carry):
        exchange_one(k)
        exchange_two(k - 1)
        pl.when(k + 1 < heads)(functools.partial(relay, k + 1))
        start_head(k - 2)
        finish_head(k - 2)
        return carry

    lax.fori_loop(2, heads, step, 0)
    exchange_two(heads - 1)
    for k in range(front, heads):
        tiles = parents_of(k)
        for j in range(local):
            tail[k - front, j] = tiles[j]

    def finish(k, carry):
        for d in range(1, nz):
            when_direct(d, z_copy(k, d).wait_send)
        for who, source, target in ends:
            pl.when(my_z == who)(relay_copy(k, source, target).wait_send)
        c_copy(k).wait_send()
        if ny > 1:
            y_copy(k).wait_send()
        return carry

    lax.fori_loop(0, heads, finish, 0)

    def stored(k, carry):
        store(k, k, obuf, out_hbm, osem).wait()
        return carry

    lax.fori_loop(0, front, stored, 0)

    def r_finish(d, carry):
        r_arrival(d).wait_recv()
        r_copy(d).wait_send()
        return carry

    lax.fori_loop(1, n, r_finish, 0)


def halves(heads):
    return [(k, 0, 2) for k in range(heads)]


def plane_kernel(
    nz, row_hbm, prm_hbm, head_hbm, kv_hbm, q_hbm, nk_hbm, nv_hbm,
    obuf, shares, qlast, klast, vlast, *scratch
):
    local, _, step_len, kv_width = kv_hbm.shape
    heads = kv_width // HEAD_SIZE
    chunks = halves(heads)
    raws = scratch[:len(chunks)]
    (
        kept, picked, share, held, qbuf, kbuf, vbuf, rbuf,
        row, prm, head, kv, crow, listed, code,
        rsend, rrecv, asend, arecv, zsend, zrecv, fsend, frecv, psend,
        msend, mrecv, isem, csem,
    ) = scratch[len(chunks):]
    me = lax.axis_index("beam")
    plane = kept.shape[1]
    n = nz * plane
    rows = step_len // plane
    new_len = q_hbm.shape[1]
    front = qbuf.shape[0]
    hbm = (q_hbm, nk_hbm, nv_hbm)
    buf = (qbuf, kbuf, vbuf, obuf)
    my_q = lax.rem(me, plane)
    my_z = lax.div(me, plane)
    inner = (my_z == 1) | (my_z == 2)
    outer = jnp.logical_not(inner)
    near = jnp.where(my_z < 2, 1 - my_z, 5 - my_z)
    my_rows = pl.ds(pl.multiple_of(my_q * rows, rows), rows)

    inputs = [
        pltpu.make_async_copy(src, dst, csem.at[i])
        for i, (src, dst) in enumerate(
            [(row_hbm, listed), (kv_hbm, kv), (row_hbm, row), (prm_hbm, prm), (head_hbm, head)]
        )
    ]
    for copy in inputs:
        copy.start()

    barrier = pltpu.get_barrier_semaphore()

    def greet(d, carry):
        pl.semaphore_signal(
            barrier, inc=1, device_id={"beam": lax.rem(me + d, n)},
            device_id_type=pl.DeviceIdType.MESH,
        )
        return carry

    lax.fori_loop(1, n, greet, 0)

    inputs[0].wait()
    low, high = local - 1, 0
    for c in range(listed.shape[1]):
        spot = listed[0, c] - me * local
        mine = (spot >= 0) & (spot < local)
        low = jnp.where(mine, jnp.minimum(low, spot), low)
        high = jnp.where(mine, jnp.maximum(high, spot), high)
    inputs[1].wait()

    def keep(c):
        k, lo, count = chunks[c]
        cols = slice(k * HEAD_SIZE, (k + 1) * HEAD_SIZE)
        part = slice(lo, lo + count)
        for r, beam in enumerate((low, high)):
            raws[c][me * KEEP + r] = kv[beam, part, my_rows, cols]
            for q in range(plane):
                kept[k, q, r, part] = kv[beam, part, q * rows:(q + 1) * rows, cols]

    keep(0)
    pl.semaphore_wait(barrier, n - 1)

    def mate(d):
        if d == 1:
            return my_q + 1 - 2 * lax.rem(my_q, 2)
        return lax.rem(my_q + 2, plane) if d == 2 else plane - 1 - my_q

    def a_part(c, q, source):
        k, lo, count = chunks[c]
        slot = pl.ds((my_z * plane + source) * KEEP, KEEP)
        return kept.at[k, q, :, pl.ds(lo, count)], raws[c].at[slot]

    def a_copy(c, d):
        src, dst = a_part(c, mate(d), my_q)
        return remote(
            src, dst, asend.at[c, d], arecv.at[c, my_q], my_z * plane + mate(d)
        )

    def a_arrival(c, d):
        src, dst = a_part(c, mate(d), mate(d))
        return remote(
            src, dst, asend.at[c, d], arecv.at[c, mate(d)], my_z * plane + mate(d)
        )

    def z_copy(c, i, target):
        slot = pl.ds(my_z * plane * KEEP, plane * KEEP)
        return remote(
            raws[c].at[slot], raws[c].at[slot], zsend.at[c, i], zrecv.at[c, my_z],
            target * plane + my_q,
        )

    def z_arrival(c, d):
        z = lax.rem(my_z + d, nz)
        slot = pl.ds(z * plane * KEEP, plane * KEEP)
        return remote(
            raws[c].at[slot], raws[c].at[slot], zsend.at[c, 0], zrecv.at[c, z],
            z * plane + my_q,
        )

    def f_copy(q, i, target):
        slot = pl.ds((my_z * plane + q) * KEEP, KEEP)
        return remote(
            raws[0].at[slot], raws[0].at[slot], fsend.at[i, q], frecv.at[my_z, q],
            target * plane + my_q,
        )

    def f_arrival(d, q):
        z = lax.rem(my_z + d, nz)
        slot = pl.ds((z * plane + q) * KEEP, KEEP)
        return remote(
            raws[0].at[slot], raws[0].at[slot], fsend.at[0, q], frecv.at[z, q],
            z * plane + my_q,
        )

    def along(do):
        @pl.when(outer)
        def _():
            do(0, nz - 1 - near)
            do(1, near)

        @pl.when(inner)
        def _():
            do(0, nz - 1 - my_z)

    def slices(c, source):
        k, lo, count = chunks[c]
        part = pl.ds(lo, count)
        return k, part, held.at[k, source, :, part]

    def p_copy(c, q):
        k, part, dst = slices(c, my_q)
        return remote(
            picked.at[k, pl.ds(q * local, local), part], dst,
            psend.at[c, q], mrecv.at[c, my_q], near * plane + q,
        )

    def p_arrival(c, q):
        k, part, dst = slices(c, q)
        return remote(
            picked.at[k, pl.ds(q * local, local), part], dst,
            psend.at[c, q], mrecv.at[c, q], near * plane + q,
        )

    def m_copy(c, d):
        k, part, dst = slices(c, my_q)
        q = mate(d)
        return remote(
            share.at[k, pl.ds(q * local, local), part], dst,
            msend.at[c, d], mrecv.at[c, my_q], my_z * plane + q,
        )

    def m_arrival(c, d):
        q = mate(d)
        k, part, dst = slices(c, q)
        return remote(
            share.at[k, pl.ds(q * local, local), part], dst,
            msend.at[c, d], mrecv.at[c, q], my_z * plane + q,
        )

    def r_copy(d):
        return remote(
            rbuf.at[me], rbuf.at[me], rsend.at[d], rrecv.at[my_q],
            my_z * plane + mate(d),
        )

    def r_arrival(d):
        src = my_z * plane + mate(d)
        return remote(rbuf.at[src], rbuf.at[src], rsend.at[d], rrecv.at[mate(d)], src)

    def s_copy(d):
        block = rbuf.at[pl.ds(my_z * plane, plane)]
        return remote(
            block, block, rsend.at[plane + d], rrecv.at[plane + my_z],
            lax.rem(my_z + d, nz) * plane + my_q,
        )

    def s_arrival(d):
        z = lax.rem(my_z + d, nz)
        block = rbuf.at[pl.ds(z * plane, plane)]
        return remote(
            block, block, rsend.at[plane + d], rrecv.at[plane + z], z * plane + my_q
        )

    def a_start(c):
        for d in range(1, plane):
            a_copy(c, d).start()

    along(lambda i, target: f_copy(my_q, i, target).start())
    a_start(0)
    for c in range(1, len(chunks)):
        keep(c)
        a_start(c)
    inputs[2].wait()
    ids = row[...]
    owner = lax.div(ids, local)
    groups = lax.broadcasted_iota(jnp.int32, (n, ids.shape[1]), 0)
    own = groups == owner
    first = jnp.min(jnp.where(own, ids, n * local), axis=1, keepdims=True)
    first = jnp.min(jnp.where(own, first, n * local), axis=0, keepdims=True)
    crow[...] = owner * KEEP + (ids > first).astype(jnp.int32)
    numbers = pltpu.make_async_copy(crow, code, csem.at[len(inputs)])
    numbers.start()

    def last_loads():
        return loads(0, heads - 1, hbm, (qlast, klast, vlast, None), isem.at[pl.ds(front, 1)])

    def load(k, carry):
        for copy in loads(k, k, hbm, buf, isem):
            copy.start()
        return carry

    lax.fori_loop(0, front, load, 0)
    for copy in last_loads():
        copy.start()

    inputs[3].wait()
    inputs[4].wait()
    hidden = prm[...].astype(jnp.float32)
    square = jnp.mean(hidden * hidden, axis=-1, keepdims=True)
    normed = hidden * lax.rsqrt(square + 1e-05)
    score = jnp.sum(normed * head[...], axis=-1, keepdims=True)
    reward = (1.0 / (1.0 + jnp.exp(-score))).astype(jnp.bfloat16).astype(jnp.float32)
    rbuf[me] = jnp.broadcast_to(reward, (local, 128))


    def pass_on(c):
        k, lo, count = chunks[c]
        part = slice(lo, lo + count)

        @pl.when(inner)
        def _():
            for d in range(1, nz):
                if c == 0:
                    for q in range(plane):
                        f_arrival(d, q).wait_recv()
                else:
                    z_arrival(c, d).wait_recv()
            for q in range(plane):
                for t in range(q * local, (q + 1) * local):
                    picked[k, t, part] = raws[c][code[0, near * plane * local + t]]
                p_copy(c, q).start()
            for t in range(plane * local):
                share[k, t, part] = raws[c][code[0, my_z * plane * local + t]]
            for d in range(1, plane):
                m_copy(c, d).start()
            held[k, my_q, :, part] = share[k, pl.ds(my_q * local, local), part]

    def arrived(c):
        @pl.when(inner)
        def _():
            for d in range(1, plane):
                m_arrival(c, d).wait_recv()

        @pl.when(outer)
        def _():
            for q in range(plane):
                p_arrival(c, q).wait_recv()

    def place(k, keys, values):
        for j in range(local):
            for q in range(plane):
                span = slice(new_len + q * rows, new_len + (q + 1) * rows)
                keys[j, span] = held[k, q, j, 0]
                values[j, span] = held[k, q, j, 1]

    def begin(k):
        for copy in loads(k, k, hbm, buf, isem):
            copy.wait()
        place(k, kbuf.at[k], vbuf.at[k])

    def attend_some(k, lo, hi):
        def one(j, inside):
            attend(k, j, buf)
            return inside

        lax.fori_loop(lo, hi, one, 0, unroll=True)

    for d in range(1, plane):
        a_arrival(0, d).wait_recv()
        along(lambda i, target: f_copy(mate(d), i, target).start())

    def z_start(c):
        for d in range(1, plane):
            a_arrival(c, d).wait_recv()
        along(lambda i, target: z_copy(c, i, target).start())

    for c in range(1, 3):
        z_start(c)
    numbers.wait()
    pass_on(0)
    for c in range(3, 5):
        z_start(c)
    for d in range(1, plane):
        r_copy(d).start()
    pass_on(1)
    for c in range(5, len(chunks)):
        z_start(c)
    for d in range(1, plane):
        r_arrival(d).wait_recv()
        r_copy(d).wait_send()
    for d in range(1, nz):
        s_copy(d).start()

    def step(k, carry):
        for c in range(2, heads):
            pl.when(k + 2 == c)(functools.partial(pass_on, c))
        for c in range(front):
            pl.when(k == c)(functools.partial(arrived, c))
        begin(k)
        attend_some(k, 0, local)
        return carry

    lax.fori_loop(0, front, step, 0)

    for d in range(1, nz):
        s_arrival(d).wait_recv()
        s_copy(d).wait_send()
    reward = rbuf[:, :, :ids.shape[1]]
    beam = lax.broadcasted_iota(jnp.int32, reward.shape, 0) * local
    beam = beam + lax.broadcasted_iota(jnp.int32, reward.shape, 1)
    given = jnp.where(beam == row[...][None], reward, 0.0)
    given = jnp.sum(jnp.sum(given, axis=0), axis=0, keepdims=True)
    shares[...] = ids.shape[1] * given / jnp.sum(given, axis=1, keepdims=True)

    along(lambda i, target: [f_copy(q, i, target).wait_send() for q in range(plane)])
    for c in range(len(chunks)):
        for d in range(1, plane):
            a_copy(c, d).wait_send()
        if c > 0:
            along(lambda i, target: z_copy(c, i, target).wait_send())

        @pl.when(inner)
        def _():
            for q in range(plane):
                p_copy(c, q).wait_send()
            for d in range(1, plane):
                m_copy(c, d).wait_send()

    for copy in last_loads():
        copy.wait()
    arrived(front)
    place(heads - 1, klast.at[0], vlast.at[0])


def close_kernel(
    shares, part, qlast, klast, vlast, out_hbm, mine, obuf, psem, osem
):
    front, local, _, width = part.shape

    def move(k):
        return pltpu.make_async_copy(
            part.at[k], out_hbm.at[:, :, pl.ds(k * width, width)], psem.at[k]
        )

    def put(j):
        return pltpu.make_async_copy(
            obuf.at[0, j], out_hbm.at[j, :, pl.ds(front * width, width)], osem.at[j]
        )

    for k in range(front):
        move(k).start()
    me = lax.axis_index("beam")
    all_shares = shares[...]
    lane = lax.broadcasted_iota(jnp.int32, all_shares.shape, 1)
    for j in range(local):
        mine[j] = jnp.sum(jnp.where(lane == me * local + j, all_shares, 0.0))
    for j in range(local):
        attend(0, j, (qlast, klast, vlast, obuf))
        put(j).start()
    for k in range(front):
        move(k).wait()
    for j in range(local):
        put(j).wait()


def plane_body(queries, new_keys, new_values, step_kv, prm_last, value_head, parents):
    n = lax.axis_size("beam")
    ny, nz = 2, 4
    plane = 2 * ny
    local, new_len, qwidth = queries.shape
    step_len, kv_width = step_kv.shape[2:]
    heads = kv_width // HEAD_SIZE
    width = qwidth // heads
    rows = step_len // plane
    front = heads - 1
    chunks = halves(heads)
    many = len(chunks)
    total = new_len + step_len
    dma = pltpu.SemaphoreType.DMA
    bf16 = jnp.bfloat16
    vmem = pl.BlockSpec(memory_space=pltpu.VMEM)
    smem = pl.BlockSpec(memory_space=pltpu.SMEM)
    in_hbm = pl.BlockSpec(memory_space=pltpu.HBM)
    anywhere = pl.BlockSpec(memory_space=pl.ANY)
    row = parents.reshape(1, -1)
    part, shares, qlast, klast, vlast = pl.pallas_call(
        functools.partial(plane_kernel, nz),
        out_shape=(
            pltpu.VMEM((front, local, new_len, width), bf16),
            pltpu.VMEM(row.shape, jnp.float32),
            pltpu.VMEM((1, local, new_len, width), bf16),
            pltpu.VMEM((1, local, total, HEAD_SIZE), bf16),
            pltpu.VMEM((1, local, total, HEAD_SIZE), bf16),
        ),
        in_specs=[in_hbm] * 7,
        out_specs=(vmem,) * 5,
        scratch_shapes=[
            pltpu.VMEM((n * KEEP, count, rows, HEAD_SIZE), bf16)
            for _, _, count in chunks
        ]
        + [
            pltpu.VMEM((heads, plane, KEEP, 2, rows, HEAD_SIZE), bf16),
            pltpu.VMEM((heads, plane * local, 2, rows, HEAD_SIZE), bf16),
            pltpu.VMEM((heads, plane * local, 2, rows, HEAD_SIZE), bf16),
            pltpu.VMEM((heads, plane, local, 2, rows, HEAD_SIZE), bf16),
            pltpu.VMEM((front, local, new_len, width), bf16),
            pltpu.VMEM((front, local, total, HEAD_SIZE), bf16),
            pltpu.VMEM((front, local, total, HEAD_SIZE), bf16),
            pltpu.VMEM((n, local, 128), jnp.float32),
            pltpu.VMEM(row.shape, jnp.int32),
            pltpu.VMEM(prm_last.shape, bf16),
            pltpu.VMEM((1, value_head.shape[0]), jnp.float32),
            pltpu.VMEM(step_kv.shape, bf16),
            pltpu.VMEM(row.shape, jnp.int32),
            pltpu.SMEM(row.shape, jnp.int32),
            pltpu.SMEM(row.shape, jnp.int32),
            dma((n,)), dma((n,)),
            dma((many, plane)), dma((many, plane)),
            dma((many, 2)), dma((many, nz)),
            dma((2, plane)), dma((nz, plane)),
            dma((many, plane)),
            dma((many, plane)), dma((many, plane)),
            dma((heads, 5)), dma((6,)),
        ],
        compiler_params=pltpu.CompilerParams(
            collective_id=0, has_side_effects=True, vmem_limit_bytes=44 << 20
        ),
    )(
        *(
            pltpu.with_memory_space_constraint(x, pltpu.HBM)
            for x in (row, prm_last, value_head.reshape(1, -1), step_kv)
        ),
        queries, new_keys, new_values,
    )
    return pl.pallas_call(
        close_kernel,
        out_shape=(
            jax.ShapeDtypeStruct(queries.shape, bf16),
            jax.ShapeDtypeStruct((local,), jnp.float32),
        ),
        in_specs=[vmem] * 5,
        out_specs=(anywhere, smem),
        scratch_shapes=[
            pltpu.VMEM((1, local, new_len, width), bf16),
            dma((front,)), dma((local,)),
        ],
        compiler_params=pltpu.CompilerParams(vmem_limit_bytes=24 << 20),
    )(shares, part, qlast, klast, vlast)


def line_body(queries, new_keys, new_values, step_kv, prm_last, value_head, parents):
    n = lax.axis_size("beam")
    ny = 1
    nz = n // (2 * ny)
    me = lax.axis_index("beam")
    local, new_len, qwidth = queries.shape
    children = parents.shape[0]
    step_len, kv_width = step_kv.shape[2:]
    heads = kv_width // HEAD_SIZE
    width = qwidth // heads

    beams = jnp.arange(n * local, dtype=jnp.int32)
    equal = parents[None, :] == beams[:, None]
    hits = jnp.sum(equal.astype(jnp.int32), axis=1)
    kept = (hits > 0).astype(jnp.int32)
    before = jnp.sum(kept[None, :] * (beams[None, :] < beams[:, None]), axis=1)
    rank_of_beam = before % KEEP
    wanted = (
        (beams[None, :] // local == me)
        & (kept[None, :] > 0)
        & (rank_of_beam[None, :] == jnp.arange(KEEP, dtype=jnp.int32)[:, None])
    )
    keep_pos = jnp.sum(wanted * (beams % local)[None, :], axis=1).astype(jnp.int32)
    rank = jnp.sum(equal * rank_of_beam[:, None], axis=0)
    owner = parents // local
    c, y, z = owner % 2, (owner // 2) % ny, owner // (2 * ny)
    my_c, my_y = me % 2, (me // 2) % ny
    code = jnp.where(y == my_y, ((c != my_c) * nz + z) * KEEP + rank, -1).astype(jnp.int32)
    y_peer = me + 2 - 4 * my_y if ny > 1 else me
    own = lax.dynamic_slice_in_dim(code, me * local, local)
    other = lax.dynamic_slice_in_dim(code, y_peer * local, local)
    idx = jnp.concatenate([keep_pos, own, other])

    dma = pltpu.SemaphoreType.DMA
    bf16 = jnp.bfloat16
    vmem = pl.BlockSpec(memory_space=pltpu.VMEM)
    anywhere = pl.BlockSpec(memory_space=pl.ANY)
    last = 2
    front = heads - last
    part, rewards, tail = pl.pallas_call(
        functools.partial(kernel, n, ny, nz),
        out_shape=(
            jax.ShapeDtypeStruct((local, new_len, front * width), bf16),
            jax.ShapeDtypeStruct((n, local, 128), jnp.float32),
            jax.ShapeDtypeStruct((last, local, 2, step_len, HEAD_SIZE), bf16),
        ),
        in_specs=[pl.BlockSpec(memory_space=pltpu.SMEM), vmem, vmem, vmem]
        + [anywhere] * 3,
        out_specs=(anywhere, vmem, vmem),
        scratch_shapes=[
            pltpu.VMEM((heads, 2, nz, KEEP, 2, step_len, HEAD_SIZE), bf16),
            pltpu.VMEM((heads, local, 2, step_len, HEAD_SIZE), bf16),
            pltpu.VMEM((heads, local, 2, step_len, HEAD_SIZE), bf16),
            pltpu.VMEM((front, local, new_len, width), bf16),
            pltpu.VMEM((front, local, new_len + step_len, HEAD_SIZE), bf16),
            pltpu.VMEM((front, local, new_len + step_len, HEAD_SIZE), bf16),
            pltpu.VMEM((front, local, new_len, width), bf16),
            dma((n,)), dma((n,)),
            dma((heads, nz)), dma((heads, nz)), dma((heads,)),
            dma((heads,)), dma((heads,)),
            dma((heads,)), dma((heads,)),
            dma((front, 5)), dma((front,)),
        ],
        compiler_params=pltpu.CompilerParams(
            collective_id=0, has_side_effects=True, vmem_limit_bytes=56 << 20
        ),
    )(idx, prm_last, value_head.reshape(1, -1), step_kv, queries, new_keys, new_values)

    attended = pl.pallas_call(
        functools.partial(last_kernel, front),
        out_shape=jax.ShapeDtypeStruct(queries.shape, bf16),
        in_specs=[vmem] + [anywhere] * 4,
        out_specs=anywhere,
        scratch_shapes=[
            pltpu.VMEM((last, local, new_len, width), bf16),
            pltpu.VMEM((last, local, new_len + step_len, HEAD_SIZE), bf16),
            pltpu.VMEM((last, local, new_len + step_len, HEAD_SIZE), bf16),
            pltpu.VMEM((last, local, new_len, width), bf16),
            pltpu.VMEM((local, new_len, front * width), bf16),
            dma((last, 5)), dma((last,)), dma((local,)), dma((local,)),
        ],
        compiler_params=pltpu.CompilerParams(vmem_limit_bytes=56 << 20),
    )(tail, part, queries, new_keys, new_values)

    reward = rewards[:, :, 0].reshape(-1)
    total = jnp.sum(reward * hits.astype(jnp.float32))
    mine = lax.dynamic_slice_in_dim(parents, me * local, local)
    match = mine[:, None] == beams[None, :]
    child_reward = jnp.sum(jnp.where(match, reward[None, :], 0.0), axis=1)
    child_share = children * child_reward / total
    return (attended, child_share)


def solution(mesh):
    in_specs = (
        P(("prompts", "beam"), None, None),
        P(("prompts", "beam"), None, None),
        P(("prompts", "beam"), None, None),
        P(("prompts", "beam"), None, None, None),
        P(("prompts", "beam"), None),
        P(),
        P("prompts"),
    )
    out_specs = (P(("prompts", "beam"), None, None), P(("prompts", "beam")))
    body = plane_body if mesh.shape["beam"] == 16 else line_body
    return jax.shard_map(body, mesh=mesh, in_specs=in_specs, out_specs=out_specs, check_vma=False)
```
